128 devices in a mesh: site: 8 (over x, core), sec: 16 (over z, y).
Axes of the slice: x: 4, y: 4, z: 4, core: 2. Of those that a mesh axis runs over, the one named last changes fastest.
Arguments:
- tensors: bfloat16 [8, 32, 4, 512, 512], P('site', 'sec'), as said below
- factors: float32 [8, 32, 512, 512], P('site', 'sec'), as said below
- sector_sizes: int32 [8, 32], replicated, may hold values from 384 to 512, as said below
- merging: int32 [8, 32, 4], replicated, may hold values from 0 to 31, as said below
Outputs:
- isometry: float32 [8, 32, 4, 512, 512], P('site', 'sec')
- factor_out: float32 [8, 32, 512, 512], P('site', 'sec')
The draws below stay inside these ranges and needn't reach their ends.
Inputs may be any that keep to these rules, and one draw needn't show every extreme that they name: `sector_sizes`: every bond has one sector of exactly 512 states and one of exactly 384. For every site and physical state, merging maps the left sectors one to one onto the right sectors; the 8 blocks (left sector, physical state) of the left sectors that lie on one index of sec go to 8 different indices of sec, one block to each. `tensors`: zero outside the rows below the left sector's size and the columns below the right sector's size. `factors`: upper triangular with a positive diagonal inside the sector's size, the identity on its padding.
All inputs are finite; a program needn't handle non-finite values.
Results may differ from the reference program's by a relative error of at most 0.007.
Values may be sent and summed in bfloat16 or wider, within the bound.
No kernel may reach another device: no remote copies, remote signals or barrier semaphores. Data moves between devices by JAX's collectives and lax.ppermute only.
A program may use at most 192 MiB of HBM per device.

```python
import math
import jax
import jax.numpy as jnp
from jax import lax

BLK = 512
PHYS = 4
SEC_DEV = 2
ROUNDS = 3
NSEC = 32
SITES = 8


def sector_widths(key):
    key_base, key_first, key_second = jax.random.split(jax.random.fold_in(key, 101), 3)
    drawn_widths = jax.random.randint(key_base, (SITES, NSEC), 3 * BLK // 4, BLK + 1)
    first_pos = jax.random.randint(key_first, (SITES,), 0, NSEC)
    second_pos = (first_pos + 1 + jax.random.randint(key_second, (SITES,), 0, NSEC - 1)) % NSEC
    columns = jnp.arange(NSEC, dtype=jnp.int32)[None, :]
    drawn_widths = jnp.where(columns == first_pos[:, None], BLK, drawn_widths)
    drawn_widths = jnp.where(columns == second_pos[:, None], 3 * BLK // 4, drawn_widths)
    return drawn_widths.astype(jnp.int32)


def one_site_table(site_key):
    groups = NSEC // SEC_DEV
    key_first, key_second, key_offset, key_turn = jax.random.split(site_key, 4)
    first_perm = jax.random.permutation(key_first, groups)
    second_perm = jax.random.permutation(key_second, groups)
    offsets = jax.random.permutation(key_offset, groups)[:SEC_DEV * PHYS]
    turned = jax.random.randint(key_turn, (PHYS, groups), 0, SEC_DEV)
    columns_out = []
    for phys_index in range(PHYS):
        inner_cols = []
        for inner in range(SEC_DEV):
            dest_dev = second_perm[(first_perm + offsets[inner * PHYS + phys_index]) % groups]
            turn_here = turned[phys_index][dest_dev]
            inner_cols.append(dest_dev * SEC_DEV + (inner + turn_here) % SEC_DEV)
        columns_out.append(jnp.stack(inner_cols, axis=1).reshape(NSEC))
    return jnp.stack(columns_out, axis=-1).astype(jnp.int32)


def merging_table(key):
    site_keys = jax.random.split(jax.random.fold_in(key, 202), SITES)
    return jax.vmap(one_site_table)(site_keys)


def draw_sector_sizes(key, part):
    return sector_widths(key)


def draw_merging(key, part):
    return merging_table(key)


def draw_tensors(key, part):
    widths = sector_widths(key)
    table = merging_table(key)
    key_values = jax.random.fold_in(jax.random.fold_in(key, 303), 0)
    spread_scale = (PHYS * BLK) ** (-0.5)
    full_shape = (SITES, NSEC, PHYS, BLK, BLK)
    values_drawn = jax.random.normal(key_values, full_shape, jnp.float32) * spread_scale
    next_widths = jnp.roll(widths, -1, axis=0)
    selector = (table[..., None] == jnp.arange(NSEC, dtype=jnp.int32)).astype(jnp.int32)
    column_widths = jnp.sum(selector * next_widths[:, None, None, :], axis=-1)
    positions = jnp.arange(BLK, dtype=jnp.int32)
    rows_inside = positions[None, None, None, :, None] < widths[:, :, None, None, None]
    columns_inside = positions[None, None, None, None, :] < column_widths[:, :, :, None, None]
    return jnp.where(rows_inside & columns_inside, values_drawn, 0.0).astype(jnp.bfloat16)


def draw_factors(key, part):
    widths = sector_widths(key)
    key_diag, key_upper = jax.random.split(jax.random.fold_in(key, 404))
    full_shape = (SITES, NSEC, BLK, BLK)
    diagonal = jnp.exp(jax.random.uniform(key_diag, (SITES, NSEC, BLK, 1), jnp.float32, math.log(0.5), math.log(2.0)))
    upper_vals = jax.random.normal(key_upper, full_shape, jnp.float32) * (0.5 / math.sqrt(BLK))
    positions = jnp.arange(BLK, dtype=jnp.int32)
    row_inside = positions[None, None, :, None] < widths[:, :, None, None]
    column_inside = positions[None, None, None, :] < widths[:, :, None, None]
    on_diagonal = positions[:, None] == positions[None, :]
    above = positions[:, None] < positions[None, :]
    inside = row_inside & column_inside
    result = jnp.where(on_diagonal[None, None] & inside, diagonal, 0.0)
    result = jnp.where(above[None, None] & inside, upper_vals, result)
    result = jnp.where(on_diagonal[None, None] & jnp.logical_not(inside), 1.0, result)
    return result.astype(jnp.float32)


def setup_inputs(seed: int = 0) -> dict:
    key_list = jax.random.split(jax.random.key(seed), 5)
    return {
        "tensors": draw_tensors(jax.random.fold_in(key_list[4], 71), 0),
        "factors": draw_factors(jax.random.fold_in(key_list[4], 71), 0),
        "sector_sizes": draw_sector_sizes(jax.random.fold_in(key_list[4], 71), 0),
        "merging": draw_merging(jax.random.fold_in(key_list[4], 71), 0),
    }


HIGH = lax.Precision.HIGHEST

def stack_site(inputs):
    blocks, carried, merging_rows, widths = inputs
    left_factor = carried.astype(jnp.bfloat16).astype(jnp.float32)
    products = jnp.einsum('ajk,apkl->apjl', left_factor, blocks.astype(jnp.float32), precision=HIGH).astype(jnp.bfloat16)
    selector = (merging_rows[:, :, None] == jnp.arange(NSEC, dtype=jnp.int32)[None, None, :]).astype(jnp.float32)
    stacked = jnp.einsum('apb,apjl->bpjl', selector, products.astype(jnp.float32), precision=HIGH)
    stacked = stacked.reshape(NSEC, PHYS * BLK, BLK)
    gram_matrix = jnp.einsum('brl,brm->blm', stacked, stacked, precision=HIGH)
    padding = (jnp.arange(BLK, dtype=jnp.int32)[None, :] >= widths[:, None]).astype(jnp.float32)
    gram_matrix = gram_matrix + jnp.eye(BLK, dtype=jnp.float32)[None] * padding[:, None, :]
    lower_factor = jnp.linalg.cholesky(gram_matrix)
    return (lower_factor, stacked)

def factor_site(inputs):
    lower_factor, stacked = stack_site(inputs)
    return jnp.swapaxes(lower_factor, -1, -2)

def final_site(inputs):
    lower_factor, stacked = stack_site(inputs)
    solved = lax.linalg.triangular_solve(lower_factor, stacked, left_side=False, lower=True, transpose_a=True)
    scaled = (solved * math.sqrt(PHYS * BLK)).reshape(NSEC, PHYS, BLK, BLK)
    return (jnp.swapaxes(lower_factor, -1, -2), scaled)

def reference(tensors, factors, sector_sizes, merging):
    widths = jnp.roll(sector_sizes, -1, axis=0)
    carried = factors
    for step_index in range(ROUNDS - 1):
        upper_factor = lax.map(factor_site, (tensors, carried, merging, widths))
        carried = jnp.roll(upper_factor, 1, axis=0)
    upper_out, isometry = lax.map(final_site, (tensors, carried, merging, widths))
    return (isometry, upper_out)
```

```python
import functools
import math

import jax
import jax.numpy as jnp
from jax import lax
from jax.experimental import pallas as pl
from jax.experimental.pallas import tpu as pltpu
from jax.sharding import PartitionSpec as P

ROUNDS = 3
F32 = jnp.float32
BF16 = jnp.bfloat16
TILE = 128
HIGHEST = lax.Precision.HIGHEST


def contract(left, right, left_dim, right_dim, precision=None):
    dims = (((left_dim,), (right_dim,)), ((), ()))
    return lax.dot_general(left, right, dims, precision=precision, preferred_element_type=F32)


def from_behind(shard, axis, by):
    size = lax.axis_size(axis)
    return lax.ppermute(shard, axis, [(i, (i + by) % size) for i in range(size)])


def packed_starts(tiles):
    starts, total = [], 0
    for k in range(tiles):
        starts.append(total)
        total += tiles - k
    return starts, total


def pack_upper(square, tiles):
    pieces = []
    for k in range(tiles):
        for q in range(k, tiles):
            piece = square[k * TILE : (k + 1) * TILE, q * TILE : (q + 1) * TILE]
            pieces.append(piece.astype(BF16))
    return pieces


def place_tensor_kernel(slot_ref, block_ref, out_ref):
    out_ref[...] = block_ref[...]


def place_tensors(blocks, slots, groups):
    count, rows, columns = blocks.shape
    return pl.pallas_call(
        place_tensor_kernel,
        out_shape=jax.ShapeDtypeStruct((groups, rows, columns), blocks.dtype),
        grid_spec=pltpu.PrefetchScalarGridSpec(
            num_scalar_prefetch=1,
            grid=(count,),
            in_specs=[pl.BlockSpec((1, rows, columns), lambda g, slot: (g, 0, 0))],
            out_specs=pl.BlockSpec((1, rows, columns), lambda g, slot: (slot[g], 0, 0)),
        ),
        name="place_tensors",
    )(slots, blocks)


def place_packed(packed, slots, groups, phys_count):
    _, rows, columns = packed.shape
    count = slots.shape[0]
    return pl.pallas_call(
        place_tensor_kernel,
        out_shape=jax.ShapeDtypeStruct((groups, rows, columns), packed.dtype),
        grid_spec=pltpu.PrefetchScalarGridSpec(
            num_scalar_prefetch=1,
            grid=(count,),
            in_specs=[pl.BlockSpec((1, rows, columns), lambda g, slot: (g // phys_count, 0, 0))],
            out_specs=pl.BlockSpec((1, rows, columns), lambda g, slot: (slot[g], 0, 0)),
        ),
        name="place_packed",
    )(slots, packed)


def pack_kernel(tiles, factor_ref, out_ref):
    for index, piece in enumerate(pack_upper(factor_ref[0], tiles)):
        out_ref[0, index * TILE : (index + 1) * TILE, :] = piece


def pack_factors(factors):
    count, size, _ = factors.shape
    tiles = size // TILE
    _, total = packed_starts(tiles)
    return pl.pallas_call(
        functools.partial(pack_kernel, tiles),
        out_shape=jax.ShapeDtypeStruct((count, total * TILE, TILE), BF16),
        grid=(count,),
        in_specs=[pl.BlockSpec((1, size, size), lambda g: (g, 0, 0))],
        out_specs=pl.BlockSpec((1, total * TILE, TILE), lambda g: (g, 0, 0)),
        name="pack_factors",
    )(factors)


def product_kernel(tiles, phys_count, keep, source_ref, tensor_ref, factor_ref, gram_ref, *rest):
    starts, _ = packed_starts(tiles)
    step = pl.program_id(0)
    product_ref = rest[0]
    for k in range(tiles):
        row = jnp.concatenate(
            [
                factor_ref[0, (starts[k] + q - k) * TILE : (starts[k] + q - k + 1) * TILE, :]
                for q in range(k, tiles)
            ],
            axis=1,
        )
        part = contract(row, tensor_ref[0, k * TILE :, :], 1, 0)
        product_ref[0, k * TILE : (k + 1) * TILE, :] = part.astype(BF16)
    product = product_ref[0]
    gram = contract(product, product, 0, 0)

    @pl.when(step % phys_count == 0)
    def _():
        gram_ref[0] = gram

    @pl.when(step % phys_count != 0)
    def _():
        gram_ref[0] += gram


def products_and_gram(tensor_slots, factor_slots, sources, sec_local, phys_count, keep):
    _, size, _ = tensor_slots.shape
    _, packed_rows, _ = factor_slots.shape
    tiles = size // TILE
    count = sec_local * phys_count
    out_shape = [jax.ShapeDtypeStruct((sec_local, size, size), F32)]
    out_specs = [pl.BlockSpec((1, size, size), lambda g, source: (g // phys_count, 0, 0))]
    scratch = []
    if keep:
        out_shape.append(jax.ShapeDtypeStruct((count, size, size), BF16))
        out_specs.append(pl.BlockSpec((1, size, size), lambda g, source: (g, 0, 0)))
    else:
        scratch.append(pltpu.VMEM((1, size, size), BF16))
    return pl.pallas_call(
        functools.partial(product_kernel, tiles, phys_count, keep),
        out_shape=out_shape,
        grid_spec=pltpu.PrefetchScalarGridSpec(
            num_scalar_prefetch=1,
            grid=(count,),
            in_specs=[
                pl.BlockSpec((1, size, size), lambda g, source: (source[g], 0, 0)),
                pl.BlockSpec((1, packed_rows, TILE), lambda g, source: (source[g], 0, 0)),
            ],
            out_specs=out_specs,
            scratch_shapes=scratch,
        ),
        name="products_and_gram",
    )(sources, tensor_slots, factor_slots)


def factor_tile(stacks):
    done = [[] for _ in stacks]
    groups = TILE // 8
    for group in range(groups):
        rows = [[] for _ in stacks]
        for r in range(8):
            j = group * 8 + r
            for s, stack in enumerate(stacks):
                row = stack[group][r : r + 1, :]
                pivot = jnp.broadcast_to(row[:, j : j + 1], (1, TILE))
                rows[s].append(row * lax.rsqrt(pivot))
                if j < TILE - 1:
                    inverse = jnp.broadcast_to(1.0 / pivot, (8, TILE))
                    wide = jnp.broadcast_to(row, (8, TILE))
                    for i in range(group if r < 7 else group + 1, groups):
                        column = jnp.broadcast_to(stack[i][:, j : j + 1], (8, TILE))
                        stack[i] = stack[i] - column * wide * inverse
        for s in range(len(stacks)):
            done[s].append(jnp.concatenate(rows[s], axis=0))
    return done


def invert_tiles(uppers, row_id, column_id):
    inverses = []
    for upper in uppers:
        diagonal = jnp.sum(jnp.where(row_id == column_id, upper, 0.0), axis=0, keepdims=True)
        inverses.append(jnp.where(row_id == column_id, 1.0 / diagonal, 0.0))
    span = 1
    while span < TILE:
        pair = (row_id // (2 * span) == column_id // (2 * span)) & (
            row_id // span != column_id // span
        )
        inner = [
            contract(jnp.where(pair, upper, 0.0), inverse, 1, 0, HIGHEST)
            for upper, inverse in zip(uppers, inverses)
        ]
        inverses = [
            inverse - contract(inverse, part, 1, 0, HIGHEST)
            for inverse, part in zip(inverses, inner)
        ]
        span *= 2
    return inverses


def factor_kernel(count, tiles, final, scale, width_ref, gram_ref, *refs):
    if final:
        upper_ref, high_ref, low_ref, work, diag_inverse, full = refs
    else:
        packed_ref, work, diag_inverse = refs
        upper_ref = None
    size = tiles * TILE
    starts, _ = packed_starts(tiles)
    row_id = lax.broadcasted_iota(jnp.int32, (TILE, TILE), 0)
    column_id = lax.broadcasted_iota(jnp.int32, (TILE, TILE), 1)
    for s in range(count):
        work[s] = gram_ref[s]
        for k in range(tiles):
            lo, hi = k * TILE, (k + 1) * TILE
            on = (row_id == column_id) & (row_id + lo >= width_ref[s])
            work[s, lo:hi, lo:hi] = work[s, lo:hi, lo:hi] + jnp.where(on, 1.0, 0.0)
        if final:
            upper_ref[s] = jnp.zeros((size, size), F32)

    def step(p, carry):
        first = pl.multiple_of(p * TILE, TILE)
        stacks = []
        for s in range(count):
            stacks.append(
                [
                    work[s, pl.ds(pl.multiple_of(first + 8 * i, 8), 8), pl.ds(first, TILE)]
                    for i in range(TILE // 8)
                ]
            )
        uppers = [
            jnp.where(row_id <= column_id, jnp.concatenate(rows, axis=0), 0.0)
            for rows in factor_tile(stacks)
        ]
        inverses = invert_tiles(uppers, row_id, column_id)
        for s in range(count):
            diag_inverse[s, pl.ds(first, TILE), :] = inverses[s]
        for k in range(tiles):

            @pl.when(p == k)
            def _(k=k):
                lo, hi = k * TILE, (k + 1) * TILE
                for s in range(count):
                    if final:
                        upper_ref[s, lo:hi, lo:hi] = uppers[s]
                    else:
                        at = starts[k] * TILE
                        packed_ref[s, at : at + TILE, :] = uppers[s].astype(BF16)
                    if k + 1 == tiles:
                        continue
                    panel = contract(inverses[s], work[s, lo:hi, hi:], 0, 0, HIGHEST)
                    for q in range(k + 1, tiles):
                        left = (q - k - 1) * TILE
                        piece = panel[:, left : left + TILE]
                        if final:
                            upper_ref[s, lo:hi, q * TILE : (q + 1) * TILE] = piece
                        else:
                            at = (starts[k] + q - k) * TILE
                            packed_ref[s, at : at + TILE, :] = piece.astype(BF16)
                        here = slice(q * TILE, (q + 1) * TILE)
                        work[s, here, q * TILE :] = work[s, here, q * TILE :] - contract(
                            piece, panel[:, left:], 0, 0, HIGHEST
                        )

        return carry

    lax.fori_loop(0, tiles, step, 0)
    if final:
        for s in range(count):
            full[...] = jnp.zeros((size, size), F32)
            for k in range(tiles):
                lo, hi = k * TILE, (k + 1) * TILE
                full[lo:hi, lo:hi] = diag_inverse[s, lo:hi, :]
            span = TILE
            while span < size:
                for lo in range(0, size, 2 * span):
                    mid, hi = lo + span, lo + 2 * span
                    inner = contract(
                        upper_ref[s, lo:mid, mid:hi], full[mid:hi, mid:hi], 1, 0, HIGHEST
                    )
                    full[lo:mid, mid:hi] = -contract(full[lo:mid, lo:mid], inner, 1, 0, HIGHEST)
                span *= 2
            scaled = full[...] * scale
            high = scaled.astype(BF16)
            high_ref[s] = high
            low_ref[s] = (scaled - high.astype(F32)).astype(BF16)


def factorize(gram, widths, final, scale):
    count, size, _ = gram.shape
    tiles = size // TILE
    _, total = packed_starts(tiles)
    vmem = pl.BlockSpec(memory_space=pltpu.VMEM)
    scratch = [pltpu.VMEM((count, size, size), F32), pltpu.VMEM((count, size, TILE), F32)]
    if final:
        out_shape = [jax.ShapeDtypeStruct((count, size, size), t) for t in (F32, BF16, BF16)]
        scratch.append(pltpu.VMEM((size, size), F32))
    else:
        out_shape = [jax.ShapeDtypeStruct((count, total * TILE, TILE), BF16)]
    return pl.pallas_call(
        functools.partial(factor_kernel, count, tiles, final, scale),
        out_shape=out_shape,
        in_specs=[pl.BlockSpec(memory_space=pltpu.SMEM), vmem],
        out_specs=[vmem] * len(out_shape),
        scratch_shapes=scratch,
        name="factorize_last" if final else "factorize",
    )(widths, gram)


def isometry_kernel(product_ref, high_ref, low_ref, out_ref):
    product = product_ref[0]
    out_ref[0] = contract(product, high_ref[0], 1, 0) + contract(product, low_ref[0], 1, 0)


def isometries(products, high, low, phys_count):
    count, size, _ = products.shape
    square = (1, size, size)
    return pl.pallas_call(
        isometry_kernel,
        out_shape=jax.ShapeDtypeStruct((count, size, size), F32),
        grid=(count,),
        in_specs=[
            pl.BlockSpec(square, lambda g: (g, 0, 0)),
            pl.BlockSpec(square, lambda g: (g // phys_count, 0, 0)),
            pl.BlockSpec(square, lambda g: (g // phys_count, 0, 0)),
        ],
        out_specs=pl.BlockSpec(square, lambda g: (g, 0, 0)),
        name="isometries",
    )(products, high, low)


def body(tensors, factors, sector_sizes, merging):
    site_index = lax.axis_index("site")
    sec_index = lax.axis_index("sec")
    site_count = lax.axis_size("site")
    groups = lax.axis_size("sec")
    blocks = tensors[0]
    sec_local, phys_count, size = blocks.shape[0], blocks.shape[1], blocks.shape[3]
    count = sec_local * phys_count
    rows = lax.dynamic_index_in_dim(merging, site_index, 0, keepdims=False)
    next_widths = lax.dynamic_index_in_dim(
        sector_sizes, (site_index + 1) % site_count, 0, keepdims=False
    )
    first = sec_index * sec_local
    widths = lax.dynamic_slice_in_dim(next_widths, first, sec_local)
    slots = lax.dynamic_slice_in_dim(rows, first, sec_local).reshape(count) // sec_local
    wanted = rows[None] == (first + jnp.arange(sec_local, dtype=jnp.int32))[:, None, None]
    owner = jnp.arange(rows.shape[0], dtype=jnp.int32)[None, :, None] // sec_local
    sources = jnp.sum(jnp.where(wanted, owner, 0), axis=1).reshape(count)

    def exchange(slotted):
        return lax.all_to_all(slotted, "sec", split_axis=0, concat_axis=0, tiled=True)

    tensor_slots = exchange(place_tensors(blocks.reshape(count, size, size), slots, groups))
    packed = pack_factors(factors[0])
    scale = math.sqrt(phys_count * size)
    for round_index in range(ROUNDS):
        final = round_index + 1 == ROUNDS
        factor_slots = exchange(place_packed(packed, slots, groups, phys_count))
        gram, *products = products_and_gram(
            tensor_slots, factor_slots, sources, sec_local, phys_count, final
        )
        outs = factorize(gram, widths, final, scale)
        if not final:
            packed = from_behind(outs[0], "site", 1)
    upper, high, low = outs
    isometry = isometries(products[0], high, low, phys_count)
    return isometry.reshape(1, sec_local, phys_count, size, size), upper[None]


def solution(mesh):
    in_specs = (P("site", "sec", None, None, None), P("site", "sec", None, None), P(), P())
    out_specs = (P("site", "sec", None, None, None), P("site", "sec", None, None))
    return jax.shard_map(body, mesh=mesh, in_specs=in_specs, out_specs=out_specs, check_vma=False)
```

```python
import functools
import math

import jax
import jax.numpy as jnp
from jax import lax
from jax.experimental import pallas as pl
from jax.experimental.pallas import tpu as pltpu
from jax.sharding import PartitionSpec as P

ROUNDS = 3
F32 = jnp.float32
BF16 = jnp.bfloat16
TILE = 128
HIGHEST = lax.Precision.HIGHEST


def contract(left, right, left_dim, right_dim, precision=None):
    dims = (((left_dim,), (right_dim,)), ((), ()))
    return lax.dot_general(left, right, dims, precision=precision, preferred_element_type=F32)


def from_behind(shard, axis, by):
    size = lax.axis_size(axis)
    return lax.ppermute(shard, axis, [(i, (i + by) % size) for i in range(size)])


def packed_starts(tiles):
    starts, total = [], 0
    for k in range(tiles):
        starts.append(total)
        total += tiles - k
    return starts, total


def pack_upper(square, tiles):
    pieces = []
    for k in range(tiles):
        for q in range(k, tiles):
            piece = square[k * TILE : (k + 1) * TILE, q * TILE : (q + 1) * TILE]
            pieces.append(piece.astype(BF16))
    return pieces


def place_kernel(unique, count, slot_ref, block_ref, out_ref, held, read_sem, write_sem):
    reads = [
        pltpu.make_async_copy(block_ref.at[u], held.at[u], read_sem.at[u]) for u in range(unique)
    ]
    for read in reads:
        read.start()
    writes = []
    share = count // unique
    for u in range(unique):
        reads[u].wait()
        for g in range(u * share, (u + 1) * share):
            write = pltpu.make_async_copy(held.at[u], out_ref.at[slot_ref[g]], write_sem.at[g])
            write.start()
            writes.append(write)
    for write in writes:
        write.wait()


def place(blocks, slots, groups):
    unique, rows, columns = blocks.shape
    count = slots.shape[0]
    return pl.pallas_call(
        functools.partial(place_kernel, unique, count),
        out_shape=jax.ShapeDtypeStruct((groups, rows, columns), blocks.dtype),
        in_specs=[
            pl.BlockSpec(memory_space=pltpu.SMEM),
            pl.BlockSpec(memory_space=pl.ANY),
        ],
        out_specs=pl.BlockSpec(memory_space=pl.ANY),
        scratch_shapes=[
            pltpu.VMEM(blocks.shape, blocks.dtype),
            pltpu.SemaphoreType.DMA((unique,)),
            pltpu.SemaphoreType.DMA((count,)),
        ],
        name="place",
    )(slots, blocks)


def pack_kernel(tiles, factor_ref, out_ref):
    for index, piece in enumerate(pack_upper(factor_ref[0], tiles)):
        out_ref[0, index * TILE : (index + 1) * TILE, :] = piece


def pack_factors(factors):
    count, size, _ = factors.shape
    tiles = size // TILE
    _, total = packed_starts(tiles)
    return pl.pallas_call(
        functools.partial(pack_kernel, tiles),
        out_shape=jax.ShapeDtypeStruct((count, total * TILE, TILE), BF16),
        grid=(count,),
        in_specs=[pl.BlockSpec((1, size, size), lambda g: (g, 0, 0))],
        out_specs=pl.BlockSpec((1, total * TILE, TILE), lambda g: (g, 0, 0)),
        name="pack_factors",
    )(factors)


def product_kernel(tiles, phys_count, source_ref, left_ref, tensor_ref, factor_ref, gram_ref, *rest):
    starts, _ = packed_starts(tiles)
    step = pl.program_id(0)
    product_ref = rest[0]
    for k in range(tiles):
        row = jnp.concatenate(
            [
                factor_ref[0, (starts[k] + q - k) * TILE : (starts[k] + q - k + 1) * TILE, :]
                for q in range(k, tiles)
            ],
            axis=1,
        )
        part = contract(row, tensor_ref[0, k * TILE :, :], 1, 0)
        product_ref[0, k * TILE : (k + 1) * TILE, :] = part.astype(BF16)
    first = step % phys_count == 0
    for k in range(tiles):
        here = slice(k * TILE, (k + 1) * TILE)
        part = contract(product_ref[0, :, here], product_ref[0, :, k * TILE :], 0, 0)

        @pl.when(first)
        def _(here=here, k=k, part=part):
            gram_ref[0, here, k * TILE :] = part

        @pl.when(jnp.logical_not(first))
        def _(here=here, k=k, part=part):
            gram_ref[0, here, k * TILE :] += part


def products_and_gram(tensor_slots, factor_slots, sources, lefts, sec_local, phys_count, keep):
    _, size, _ = tensor_slots.shape
    _, packed_rows, _ = factor_slots.shape
    tiles = size // TILE
    count = sec_local * phys_count
    out_shape = [jax.ShapeDtypeStruct((sec_local, size, size), F32)]
    out_specs = [pl.BlockSpec((1, size, size), lambda g, source, left: (g // phys_count, 0, 0))]
    scratch = []
    if keep:
        out_shape.append(jax.ShapeDtypeStruct((count, size, size), BF16))
        out_specs.append(pl.BlockSpec((1, size, size), lambda g, source, left: (g, 0, 0)))
    else:
        scratch.append(pltpu.VMEM((1, size, size), BF16))
    return pl.pallas_call(
        functools.partial(product_kernel, tiles, phys_count),
        out_shape=out_shape,
        grid_spec=pltpu.PrefetchScalarGridSpec(
            num_scalar_prefetch=2,
            grid=(count,),
            in_specs=[
                pl.BlockSpec((1, size, size), lambda g, source, left: (source[g], 0, 0)),
                pl.BlockSpec((1, packed_rows, TILE), lambda g, source, left: (left[g], 0, 0)),
            ],
            out_specs=out_specs,
            scratch_shapes=scratch,
        ),
        name="products_and_gram",
    )(sources, lefts, tensor_slots, factor_slots)


def factor_group(rows8, j, lane, sub):
    full = (8, TILE)
    rows = [jnp.broadcast_to(rows8[t : t + 1, :], full) for t in range(8)]
    units = [jnp.where(lane == j + t, 1.0, 0.0) for t in range(8)]
    columns = [jnp.broadcast_to(rows8[:, j + u : j + u + 1], full) for u in range(8)]
    block = [
        [jnp.broadcast_to(columns[u][t : t + 1, :], full) if u >= t else None for u in range(8)]
        for t in range(8)
    ]
    inverse, lower = [], {}
    for t in range(8):
        inverse.append(1.0 / block[t][t])
        for u in range(t + 1, 8):
            lower[u, t] = block[t][u] * inverse[t]
        for u in range(t + 1, 8):
            for v in range(u, 8):
                block[u][v] = block[u][v] - lower[u, t] * block[t][v]
    for t in range(8):
        for v in range(t):
            rows[t] = rows[t] - lower[t, v] * rows[v]
            units[t] = units[t] - lower[t, v] * units[v]
    upper = jnp.zeros(full, F32)
    unit = jnp.zeros(full, F32)
    for t in range(8):
        root = lax.rsqrt(block[t][t])
        upper = jnp.where(sub == t, rows[t] * root, upper)
        unit = jnp.where(sub == t, units[t] * root, unit)
    reduced = [rows[t] * inverse[t] for t in range(8)]
    for t in range(7, -1, -1):
        for v in range(t + 1, 8):
            reduced[t] = reduced[t] - lower[v, t] * reduced[v]
    return upper, unit, reduced


def factor_tile(stacks):
    groups, wide = TILE // 8, 4
    lane = lax.broadcasted_iota(jnp.int32, (8, TILE), 1)
    sub = lax.broadcasted_iota(jnp.int32, (8, TILE), 0)
    uppers, units = [[] for _ in stacks], [[] for _ in stacks]
    for group in range(groups):
        j = group * 8
        end = (group // wide + 1) * wide
        for s, stack in enumerate(stacks):
            upper, unit, reduced = factor_group(stack[group], j, lane, sub)
            uppers[s].append(upper)
            units[s].append(unit)
            for i in range(group + 1, end):
                total = None
                for t in range(8):
                    term = jnp.broadcast_to(stack[i][:, j + t : j + t + 1], (8, TILE)) * reduced[t]
                    total = term if total is None else total + term
                stack[i] = stack[i] - total
        if end == group + 1 and end < groups:
            for s, stack in enumerate(stacks):
                done = jnp.concatenate(uppers[s][end - wide :], axis=0)
                update = contract(done, done, 0, 0, HIGHEST)
                for i in range(end, groups):
                    stack[i] = stack[i] - update[8 * i : 8 * i + 8]
    return uppers, units


def invert_tiles(uppers, units, row_id, column_id):
    span = 8
    while span < TILE:
        pair = (row_id // (2 * span) == column_id // (2 * span)) & (
            row_id // span != column_id // span
        )
        inner = [
            contract(unit, jnp.where(pair, upper, 0.0), 1, 1, HIGHEST)
            for upper, unit in zip(uppers, units)
        ]
        units = [unit - contract(part, unit, 1, 0, HIGHEST) for unit, part in zip(units, inner)]
        span *= 2
    return units


def factor_kernel(count, tiles, final, scale, width_ref, gram_ref, *refs):
    if final:
        upper_ref, high_ref, low_ref, work, diag_inverse, full = refs
    else:
        packed_ref, work, diag_inverse = refs
        upper_ref = None
    size = tiles * TILE
    starts, _ = packed_starts(tiles)
    row_id = lax.broadcasted_iota(jnp.int32, (TILE, TILE), 0)
    column_id = lax.broadcasted_iota(jnp.int32, (TILE, TILE), 1)
    for s in range(count):
        work[s] = gram_ref[s]
        for k in range(tiles):
            lo, hi = k * TILE, (k + 1) * TILE
            on = (row_id == column_id) & (row_id + lo >= width_ref[s])
            work[s, lo:hi, lo:hi] = work[s, lo:hi, lo:hi] + jnp.where(on, 1.0, 0.0)
        if final:
            upper_ref[s] = jnp.zeros((size, size), F32)

    def step(p, carry):
        first = pl.multiple_of(p * TILE, TILE)
        stacks = []
        for s in range(count):
            stacks.append(
                [
                    work[s, pl.ds(pl.multiple_of(first + 8 * i, 8), 8), pl.ds(first, TILE)]
                    for i in range(TILE // 8)
                ]
            )
        upper_rows, unit_rows = factor_tile(stacks)
        uppers = [
            jnp.where(row_id <= column_id, jnp.concatenate(rows, axis=0), 0.0)
            for rows in upper_rows
        ]
        units = [jnp.concatenate(rows, axis=0) for rows in unit_rows]
        inverses = invert_tiles(uppers, units, row_id, column_id)
        for s in range(count):
            diag_inverse[s, pl.ds(first, TILE), :] = inverses[s]
        for k in range(tiles):

            @pl.when(p == k)
            def _(k=k):
                lo, hi = k * TILE, (k + 1) * TILE
                for s in range(count):
                    if final:
                        upper_ref[s, lo:hi, lo:hi] = uppers[s]
                    else:
                        at = starts[k] * TILE
                        packed_ref[s, at : at + TILE, :] = uppers[s].astype(BF16)
                    if k + 1 == tiles:
                        continue
                    panel = contract(inverses[s], work[s, lo:hi, hi:], 1, 0, HIGHEST)
                    for q in range(k + 1, tiles):
                        left = (q - k - 1) * TILE
                        piece = panel[:, left : left + TILE]
                        if final:
                            upper_ref[s, lo:hi, q * TILE : (q + 1) * TILE] = piece
                        else:
                            at = (starts[k] + q - k) * TILE
                            packed_ref[s, at : at + TILE, :] = piece.astype(BF16)
                        here = slice(q * TILE, (q + 1) * TILE)
                        work[s, here, q * TILE :] = work[s, here, q * TILE :] - contract(
                            piece, panel[:, left:], 0, 0, HIGHEST
                        )

        return carry

    lax.fori_loop(0, tiles, step, 0)
    if final:
        for s in range(count):
            full[...] = jnp.zeros((size, size), F32)
            for k in range(tiles):
                lo, hi = k * TILE, (k + 1) * TILE
                full[lo:hi, lo:hi] = jnp.transpose(diag_inverse[s, lo:hi, :])
            span = TILE
            while span < size:
                for lo in range(0, size, 2 * span):
                    mid, hi = lo + span, lo + 2 * span
                    inner = contract(
                        upper_ref[s, lo:mid, mid:hi], full[mid:hi, mid:hi], 1, 0, HIGHEST
                    )
                    full[lo:mid, mid:hi] = -contract(full[lo:mid, lo:mid], inner, 1, 0, HIGHEST)
                span *= 2
            scaled = full[...] * scale
            high = scaled.astype(BF16)
            high_ref[s] = high
            low_ref[s] = (scaled - high.astype(F32)).astype(BF16)


def factorize(gram, widths, final, scale):
    count, size, _ = gram.shape
    tiles = size // TILE
    _, total = packed_starts(tiles)
    vmem = pl.BlockSpec(memory_space=pltpu.VMEM)
    scratch = [pltpu.VMEM((count, size, size), F32), pltpu.VMEM((count, size, TILE), F32)]
    if final:
        out_shape = [jax.ShapeDtypeStruct((count, size, size), t) for t in (F32, BF16, BF16)]
        scratch.append(pltpu.VMEM((size, size), F32))
    else:
        out_shape = [jax.ShapeDtypeStruct((count, total * TILE, TILE), BF16)]
    return pl.pallas_call(
        functools.partial(factor_kernel, count, tiles, final, scale),
        out_shape=out_shape,
        in_specs=[pl.BlockSpec(memory_space=pltpu.SMEM), vmem],
        out_specs=[vmem] * len(out_shape),
        scratch_shapes=scratch,
        name="factorize_last" if final else "factorize",
    )(widths, gram)


def isometry_kernel(product_ref, high_ref, low_ref, out_ref):
    size = product_ref.shape[1]
    for lo in range(0, size, 2 * TILE):
        hi = lo + 2 * TILE
        left = product_ref[0, :, :hi]
        out_ref[0, :, lo:hi] = contract(left, high_ref[0, :hi, lo:hi], 1, 0) + contract(
            left, low_ref[0, :hi, lo:hi], 1, 0
        )


def isometries(products, high, low, phys_count):
    count, size, _ = products.shape
    square = (1, size, size)
    return pl.pallas_call(
        isometry_kernel,
        out_shape=jax.ShapeDtypeStruct((count, size, size), F32),
        grid=(count,),
        in_specs=[
            pl.BlockSpec(square, lambda g: (g, 0, 0)),
            pl.BlockSpec(square, lambda g: (g // phys_count, 0, 0)),
            pl.BlockSpec(square, lambda g: (g // phys_count, 0, 0)),
        ],
        out_specs=pl.BlockSpec(square, lambda g: (g, 0, 0)),
        name="isometries",
    )(products, high, low)


def body(tensors, factors, sector_sizes, merging):
    site_index = lax.axis_index("site")
    sec_index = lax.axis_index("sec")
    site_count = lax.axis_size("site")
    groups = lax.axis_size("sec")
    blocks = tensors[0]
    sec_local, phys_count, size = blocks.shape[0], blocks.shape[1], blocks.shape[3]
    count = sec_local * phys_count
    rows = lax.dynamic_index_in_dim(merging, site_index, 0, keepdims=False)
    next_widths = lax.dynamic_index_in_dim(
        sector_sizes, (site_index + 1) % site_count, 0, keepdims=False
    )
    first = sec_index * sec_local
    widths = lax.dynamic_slice_in_dim(next_widths, first, sec_local)
    slots = lax.dynamic_slice_in_dim(rows, first, sec_local).reshape(count) // sec_local
    wanted = rows[None] == (first + jnp.arange(sec_local, dtype=jnp.int32))[:, None, None]
    order = jnp.arange(rows.shape[0], dtype=jnp.int32)[None, :, None]
    lefts = jnp.sum(jnp.where(wanted, order, 0), axis=1).reshape(count)
    sources = lefts // sec_local

    def exchange(slotted):
        return lax.all_to_all(slotted, "sec", split_axis=0, concat_axis=0, tiled=True)

    packed = pack_factors(factors[0])
    factor_slots = lax.all_gather(packed, "sec", axis=0, tiled=True)
    tensor_slots = exchange(place(blocks.reshape(count, size, size), slots, groups))
    scale = math.sqrt(phys_count * size)
    which = lefts
    for round_index in range(ROUNDS):
        final = round_index + 1 == ROUNDS
        gram, *products = products_and_gram(
            tensor_slots, factor_slots, sources, which, sec_local, phys_count, final
        )
        outs = factorize(gram, widths, final, scale)
        if not final:
            packed = from_behind(outs[0], "site", 1)
            factor_slots = exchange(place(packed, slots, groups))
            which = sources
    upper, high, low = outs
    isometry = isometries(products[0], high, low, phys_count)
    return isometry.reshape(1, sec_local, phys_count, size, size), upper[None]


def solution(mesh):
    in_specs = (P("site", "sec", None, None, None), P("site", "sec", None, None), P(), P())
    out_specs = (P("site", "sec", None, None, None), P("site", "sec", None, None))
    return jax.shard_map(body, mesh=mesh, in_specs=in_specs, out_specs=out_specs, check_vma=False)
```

```python
import functools
import math

import jax
import jax.numpy as jnp
from jax import lax
from jax.experimental import pallas as pl
from jax.experimental.pallas import tpu as pltpu
from jax.sharding import PartitionSpec as P

ROUNDS = 3
F32 = jnp.float32
BF16 = jnp.bfloat16
TILE = 128
HIGHEST = lax.Precision.HIGHEST


def contract(left, right, left_dim, right_dim, precision=None):
    dims = (((left_dim,), (right_dim,)), ((), ()))
    return lax.dot_general(left, right, dims, precision=precision, preferred_element_type=F32)


def from_behind(shard, axis, by):
    size = lax.axis_size(axis)
    return lax.ppermute(shard, axis, [(i, (i + by) % size) for i in range(size)])


class Packing:
    SPARE = 16

    def __init__(self, tiles):
        self.tiles = tiles
        self.row = {}
        at = 0
        for k in range(tiles):
            for q in range(k + 1, tiles):
                self.row[k, q] = at
                at += TILE
        for pair in range(tiles // 2):
            self.row[pair] = at
            at += TILE
        self.diagonals = at
        self.rows = at + self.SPARE


def ids():
    row_id = lax.broadcasted_iota(jnp.int32, (TILE, TILE), 0)
    column_id = lax.broadcasted_iota(jnp.int32, (TILE, TILE), 1)
    return row_id, column_id


def pack_pair(even, odd, row_id, column_id):
    return jnp.where(row_id <= column_id, even, jnp.transpose(odd)).astype(BF16)


def pack_diagonals(odds, row_id, column_id):
    spare = lax.broadcasted_iota(jnp.int32, (Packing.SPARE, TILE), 0)
    rows = jnp.zeros((Packing.SPARE, TILE), F32)
    for pair, odd in enumerate(odds):
        diagonal = jnp.sum(jnp.where(row_id == column_id, odd, 0.0), axis=0, keepdims=True)
        rows = jnp.where(spare == pair, jnp.broadcast_to(diagonal, rows.shape), rows)
    return rows.astype(BF16)


def unpack_diagonals(packing, held, row_id, column_id):
    diagonals = held[packing.diagonals : packing.diagonals + Packing.SPARE, :].astype(F32)
    tiles = []
    for pair in range(packing.tiles // 2):
        at = packing.row[pair]
        both = held[at : at + TILE, :].astype(F32)
        diagonal = jnp.broadcast_to(diagonals[pair : pair + 1, :], both.shape)
        odd = jnp.where(
            row_id > column_id, both, jnp.where(row_id == column_id, diagonal, 0.0)
        )
        tiles.append(jnp.where(row_id <= column_id, both, 0.0).astype(BF16))
        tiles.append(jnp.transpose(odd).astype(BF16))
    return tiles


def start_all(copies):
    for copy in copies:
        copy.start()
    return copies


def wait_all(copies):
    for copy in copies:
        copy.wait()


def place_first_kernel(
    unique, count, tiles, slot_ref, factor_ref, block_ref, out_ref,
    square, held, packed, factor_sem, read_sem, write_sem, packed_sem,
):
    packing = Packing(tiles)
    size = tiles * TILE
    row_id, column_id = ids()
    factor_reads = start_all(
        [pltpu.make_async_copy(factor_ref.at[u], square.at[u], factor_sem.at[u]) for u in range(unique)]
    )
    reads = start_all(
        [pltpu.make_async_copy(block_ref.at[g], held.at[g], read_sem.at[g]) for g in range(count)]
    )
    writes = []
    share = count // unique
    for u in range(unique):
        factor_reads[u].wait()
        tile = {}
        for k in range(tiles):
            for q in range(k, tiles):
                tile[k, q] = square[u, k * TILE : (k + 1) * TILE, q * TILE : (q + 1) * TILE]
                if q > k:
                    at = packing.row[k, q]
                    packed[u, at : at + TILE, :] = tile[k, q].astype(BF16)
        for pair in range(tiles // 2):
            at = packing.row[pair]
            even, odd = tile[2 * pair, 2 * pair], tile[2 * pair + 1, 2 * pair + 1]
            packed[u, at : at + TILE, :] = pack_pair(even, odd, row_id, column_id)
        odds = [tile[k, k] for k in range(1, tiles, 2)]
        packed[u, packing.diagonals :, :] = pack_diagonals(odds, row_id, column_id)
    for g in range(count):
        reads[g].wait()
        slot = slot_ref[g]
        for q in range(tiles):
            writes.append(
                pltpu.make_async_copy(
                    held.at[g, :, q * TILE : (q + 1) * TILE],
                    out_ref.at[slot, q * size : (q + 1) * size, :],
                    write_sem.at[g, q],
                )
            )
            writes[-1].start()
        writes.append(
            pltpu.make_async_copy(
                packed.at[g // share],
                out_ref.at[slot, tiles * size : tiles * size + packing.rows, :],
                packed_sem.at[g],
            )
        )
        writes[-1].start()
    wait_all(writes)


def place_first(blocks, factors, slots, groups):
    count, size, _ = blocks.shape
    unique = factors.shape[0]
    tiles = size // TILE
    packing = Packing(tiles)
    anywhere = pl.BlockSpec(memory_space=pl.ANY)
    return pl.pallas_call(
        functools.partial(place_first_kernel, unique, count, tiles),
        out_shape=jax.ShapeDtypeStruct((groups, tiles * size + packing.rows, TILE), BF16),
        in_specs=[pl.BlockSpec(memory_space=pltpu.SMEM), anywhere, anywhere],
        out_specs=anywhere,
        scratch_shapes=[
            pltpu.VMEM(factors.shape, F32),
            pltpu.VMEM(blocks.shape, BF16),
            pltpu.VMEM((unique, packing.rows, TILE), BF16),
            pltpu.SemaphoreType.DMA((unique,)),
            pltpu.SemaphoreType.DMA((count,)),
            pltpu.SemaphoreType.DMA((count, tiles)),
            pltpu.SemaphoreType.DMA((count,)),
        ],
        name="place_first",
    )(slots, factors, blocks)


def place_kernel(unique, count, slot_ref, block_ref, out_ref, write_sem):
    share = count // unique
    wait_all(
        start_all(
            [
                pltpu.make_async_copy(
                    block_ref.at[g // share], out_ref.at[slot_ref[g]], write_sem.at[g]
                )
                for g in range(count)
            ]
        )
    )


def place(blocks, slots, groups):
    unique, rows, columns = blocks.shape
    count = slots.shape[0]
    return pl.pallas_call(
        functools.partial(place_kernel, unique, count),
        out_shape=jax.ShapeDtypeStruct((groups, rows, columns), blocks.dtype),
        in_specs=[
            pl.BlockSpec(memory_space=pltpu.SMEM),
            pl.BlockSpec(memory_space=pltpu.VMEM),
        ],
        out_specs=pl.BlockSpec(memory_space=pl.ANY),
        scratch_shapes=[
            pltpu.SemaphoreType.DMA((count,)),
        ],
        name="place",
    )(slots, blocks)


def factor_group(rows8, j, lane, sub):
    full = (8, TILE)
    rows = [jnp.broadcast_to(rows8[t : t + 1, :], full) for t in range(8)]
    units = [jnp.where(lane == j + t, 1.0, 0.0) for t in range(8)]
    columns = [jnp.broadcast_to(rows8[:, j + u : j + u + 1], full) for u in range(8)]
    block = [
        [jnp.broadcast_to(columns[u][t : t + 1, :], full) if u >= t else None for u in range(8)]
        for t in range(8)
    ]
    inverse, lower = [], {}
    for t in range(8):
        inverse.append(1.0 / block[t][t])
        for u in range(t + 1, 8):
            lower[u, t] = block[t][u] * inverse[t]
        for u in range(t + 1, 8):
            for v in range(u, 8):
                block[u][v] = block[u][v] - lower[u, t] * block[t][v]
    for t in range(8):
        for v in range(t):
            rows[t] = rows[t] - lower[t, v] * rows[v]
            units[t] = units[t] - lower[t, v] * units[v]
    upper = jnp.zeros(full, F32)
    unit = jnp.zeros(full, F32)
    for t in range(8):
        root = lax.rsqrt(block[t][t])
        upper = jnp.where(sub == t, rows[t] * root, upper)
        unit = jnp.where(sub == t, units[t] * root, unit)
    reduced = [rows[t] * inverse[t] for t in range(8)]
    for t in range(7, -1, -1):
        for v in range(t + 1, 8):
            reduced[t] = reduced[t] - lower[v, t] * reduced[v]
    return upper, unit, reduced


def factor_tile(stacks):
    groups, wide = TILE // 8, 4
    lane = lax.broadcasted_iota(jnp.int32, (8, TILE), 1)
    sub = lax.broadcasted_iota(jnp.int32, (8, TILE), 0)
    uppers, units = [[] for _ in stacks], [[] for _ in stacks]
    for group in range(groups):
        j = group * 8
        end = (group // wide + 1) * wide
        for s, stack in enumerate(stacks):
            upper, unit, reduced = factor_group(stack[group], j, lane, sub)
            uppers[s].append(upper)
            units[s].append(unit)
            for i in range(group + 1, end):
                total = None
                for t in range(8):
                    term = jnp.broadcast_to(stack[i][:, j + t : j + t + 1], (8, TILE)) * reduced[t]
                    total = term if total is None else total + term
                stack[i] = stack[i] - total
        if end == group + 1 and end < groups:
            for s, stack in enumerate(stacks):
                done = jnp.concatenate(uppers[s][end - wide :], axis=0)
                update = contract(done, done, 0, 0, HIGHEST)
                for i in range(end, groups):
                    stack[i] = stack[i] - update[8 * i : 8 * i + 8]
    return uppers, units


def invert_tiles(uppers, units, row_id, column_id):
    span = 8
    while span < TILE:
        pair = (row_id // (2 * span) == column_id // (2 * span)) & (
            row_id // span != column_id // span
        )
        inner = [
            contract(unit, jnp.where(pair, upper, 0.0), 1, 1, HIGHEST)
            for upper, unit in zip(uppers, units)
        ]
        units = [unit - contract(part, unit, 1, 0, HIGHEST) for unit, part in zip(units, inner)]
        span *= 2
    return units


def round_kernel(sec_local, phys_count, tiles, shared, final, *refs):
    refs = list(refs)
    source_ref, width_ref, tensor_slots = refs[:3]
    factor_slots = tensor_slots if shared else refs[3]
    refs = refs[3 if shared else 4 :]
    outs, refs = refs[: 2 if final else 1], refs[2 if final else 1 :]
    tensors, factors, products, work, diag_inverse, tensor_sem, factor_sem = refs[:7]
    packing = Packing(tiles)
    size = tiles * TILE
    count = sec_local * phys_count
    row_id, column_id = ids()
    if final:
        isometry_ref, upper_out = outs
        upper_ref, full, staged, upper_sem, isometry_sem = refs[7:]
    else:
        packed_ref = outs[0]
    at_factor = tiles * size if shared else 0

    def tensor_copy(g, q):
        return pltpu.make_async_copy(
            tensor_slots.at[source_ref[g], q * size : (q + 1) * size, :],
            tensors.at[g, :, q * TILE : (q + 1) * TILE],
            tensor_sem.at[g, q],
        )

    def factor_copy(g):
        return pltpu.make_async_copy(
            factor_slots.at[source_ref[g], at_factor : at_factor + packing.rows, :],
            factors.at[g],
            factor_sem.at[g],
        )

    for g in range(count):
        factor_copy(g).start()
        for q in range(tiles):
            tensor_copy(g, q).start()

    def multiply(g, carry):
        factor_copy(g).wait()
        for q in range(tiles):
            tensor_copy(g, q).wait()
        held = factors.at[g]
        diagonal = unpack_diagonals(packing, held, row_id, column_id)
        for k in range(tiles):
            row = [diagonal[k]]
            for q in range(k + 1, tiles):
                at = packing.row[k, q]
                row.append(held[at : at + TILE, :])
            row = jnp.concatenate(row, axis=1) if len(row) > 1 else row[0]
            part = contract(row, tensors[g, k * TILE :, :], 1, 0)
            products[g, k * TILE : (k + 1) * TILE, :] = part.astype(BF16)
        return carry

    lax.fori_loop(0, count, multiply, 0)
    half = size // 2
    for s in range(sec_local):
        here = slice(s * phys_count, (s + 1) * phys_count)
        stacked = products[here].reshape(phys_count * size, size)
        work[s, :half, :] = contract(stacked[:, :half], stacked, 0, 0)
        work[s, half:, half:] = contract(stacked[:, half:], stacked[:, half:], 0, 0)
        for k in range(tiles):
            lo, hi = k * TILE, (k + 1) * TILE
            on = (row_id == column_id) & (row_id + lo >= width_ref[s])
            work[s, lo:hi, lo:hi] = work[s, lo:hi, lo:hi] + jnp.where(on, 1.0, 0.0)
        if final:
            upper_ref[s] = jnp.zeros((size, size), F32)

    def step(p, carry):
        first = pl.multiple_of(p * TILE, TILE)
        stacks = []
        for s in range(sec_local):
            stacks.append(
                [
                    work[s, pl.ds(pl.multiple_of(first + 8 * i, 8), 8), pl.ds(first, TILE)]
                    for i in range(TILE // 8)
                ]
            )
        upper_rows, unit_rows = factor_tile(stacks)
        uppers = [
            jnp.where(row_id <= column_id, jnp.concatenate(rows, axis=0), 0.0)
            for rows in upper_rows
        ]
        units = [jnp.concatenate(rows, axis=0) for rows in unit_rows]
        inverses = invert_tiles(uppers, units, row_id, column_id)
        if final:
            for s in range(sec_local):
                diag_inverse[s, pl.ds(first, TILE), :] = inverses[s]
        else:
            for s in range(sec_local):
                diag_inverse[s, pl.ds(first, TILE), :] = uppers[s]
        for k in range(tiles):

            @pl.when(p == k)
            def _(k=k):
                lo, hi = k * TILE, (k + 1) * TILE
                for s in range(sec_local):
                    if final:
                        upper_ref[s, lo:hi, lo:hi] = uppers[s]
                    if k + 1 == tiles:
                        continue
                    panel = contract(inverses[s], work[s, lo:hi, hi:], 1, 0, HIGHEST)
                    for q in range(k + 1, tiles):
                        left = (q - k - 1) * TILE
                        piece = panel[:, left : left + TILE]
                        if final:
                            upper_ref[s, lo:hi, q * TILE : (q + 1) * TILE] = piece
                        else:
                            at = packing.row[k, q]
                            packed_ref[s, at : at + TILE, :] = piece.astype(BF16)
                        here = slice(q * TILE, (q + 1) * TILE)
                        work[s, here, q * TILE :] = work[s, here, q * TILE :] - contract(
                            piece, panel[:, left:], 0, 0, HIGHEST
                        )

        return carry

    lax.fori_loop(0, tiles, step, 0)
    if not final:
        for s in range(sec_local):
            diagonal = [diag_inverse[s, k * TILE : (k + 1) * TILE, :] for k in range(tiles)]
            for pair in range(tiles // 2):
                at = packing.row[pair]
                packed_ref[s, at : at + TILE, :] = pack_pair(
                    diagonal[2 * pair], diagonal[2 * pair + 1], row_id, column_id
                )
            packed_ref[s, packing.diagonals :, :] = pack_diagonals(
                diagonal[1::2], row_id, column_id
            )
        return
    uppers_out = start_all(
        [
            pltpu.make_async_copy(upper_ref.at[s], upper_out.at[s], upper_sem.at[s])
            for s in range(sec_local)
        ]
    )
    scale = math.sqrt(phys_count * size)
    isometry_out = []
    for s in range(sec_local):
        inverse = full.at[s]
        for k in range(tiles):
            lo, hi = k * TILE, (k + 1) * TILE
            inverse[lo:hi, lo:hi] = jnp.transpose(diag_inverse[s, lo:hi, :])
            if k % 2 == 1:
                inverse[lo:hi, lo - TILE : lo] = jnp.zeros((TILE, TILE), F32)
        span = TILE
        while span < size:
            for lo in range(0, size, 2 * span):
                mid, hi = lo + span, lo + 2 * span
                inner = contract(
                    upper_ref[s, lo:mid, mid:hi], inverse[mid:hi, mid:hi], 1, 0, HIGHEST
                )
                inverse[lo:mid, mid:hi] = -contract(inverse[lo:mid, lo:mid], inner, 1, 0, HIGHEST)
                if span > TILE:
                    inverse[mid:hi, lo:mid] = jnp.zeros((span, span), F32)
            span *= 2
    for s in range(sec_local):
        scaled = full[s] * scale
        high = scaled.astype(BF16)
        low = (scaled - high.astype(F32)).astype(BF16)
        for p in range(phys_count):
            g = s * phys_count + p
            for lo in range(0, size, 2 * TILE):
                hi = lo + 2 * TILE
                left = products[g, :, :hi]
                staged[g, :, lo:hi] = contract(left, high[:hi, lo:hi], 1, 0) + contract(
                    left, low[:hi, lo:hi], 1, 0
                )
            isometry_out.append(
                pltpu.make_async_copy(staged.at[g], isometry_ref.at[g], isometry_sem.at[g])
            )
            isometry_out[-1].start()
    wait_all(uppers_out + isometry_out)


def run_round(sources, widths, tensor_slots, factor_slots, sec_local, phys_count, size, final):
    tiles = size // TILE
    packing = Packing(tiles)
    count = sec_local * phys_count
    anywhere = pl.BlockSpec(memory_space=pl.ANY)
    smem = pl.BlockSpec(memory_space=pltpu.SMEM)
    shared = factor_slots is None
    operands = [sources, widths, tensor_slots] + ([] if shared else [factor_slots])
    scratch = [
        pltpu.VMEM((count, size, size), BF16),
        pltpu.VMEM((count, packing.rows, TILE), BF16),
        pltpu.VMEM((count, size, size), BF16),
        pltpu.VMEM((sec_local, size, size), F32),
        pltpu.VMEM((sec_local, size, TILE), F32),
        pltpu.SemaphoreType.DMA((count, tiles)),
        pltpu.SemaphoreType.DMA((count,)),
    ]
    if final:
        out_shape = [
            jax.ShapeDtypeStruct((count, size, size), F32),
            jax.ShapeDtypeStruct((sec_local, size, size), F32),
        ]
        out_specs = [anywhere, anywhere]
        scratch += [
            pltpu.VMEM((sec_local, size, size), F32),
            pltpu.VMEM((sec_local, size, size), F32),
            pltpu.VMEM((count, size, size), F32),
            pltpu.SemaphoreType.DMA((sec_local,)),
            pltpu.SemaphoreType.DMA((count,)),
        ]
    else:
        out_shape = [jax.ShapeDtypeStruct((sec_local, packing.rows, TILE), BF16)]
        out_specs = [pl.BlockSpec(memory_space=pltpu.VMEM)]
    return pl.pallas_call(
        functools.partial(round_kernel, sec_local, phys_count, tiles, shared, final),
        out_shape=out_shape,
        in_specs=[smem, smem] + [anywhere] * (len(operands) - 2),
        out_specs=out_specs,
        scratch_shapes=scratch,
        name="last_round" if final else "round",
    )(*operands)


def body(tensors, factors, sector_sizes, merging):
    site_index = lax.axis_index("site")
    sec_index = lax.axis_index("sec")
    site_count = lax.axis_size("site")
    groups = lax.axis_size("sec")
    blocks = tensors[0]
    sec_local, phys_count, size = blocks.shape[0], blocks.shape[1], blocks.shape[3]
    count = sec_local * phys_count
    rows = lax.dynamic_index_in_dim(merging, site_index, 0, keepdims=False)
    next_widths = lax.dynamic_index_in_dim(
        sector_sizes, (site_index + 1) % site_count, 0, keepdims=False
    )
    first = sec_index * sec_local
    widths = lax.dynamic_slice_in_dim(next_widths, first, sec_local)
    slots = lax.dynamic_slice_in_dim(rows, first, sec_local).reshape(count) // sec_local
    wanted = rows[None] == (first + jnp.arange(sec_local, dtype=jnp.int32))[:, None, None]
    order = jnp.arange(rows.shape[0], dtype=jnp.int32)[None, :, None]
    lefts = jnp.sum(jnp.where(wanted, order, 0), axis=1).reshape(count)
    sources = lefts // sec_local

    def exchange(slotted):
        return lax.all_to_all(slotted, "sec", split_axis=0, concat_axis=0, tiled=True)

    first_slots = exchange(
        place_first(blocks.reshape(count, size, size), factors[0], slots, groups)
    )
    factor_slots = None
    for round_index in range(ROUNDS):
        final = round_index + 1 == ROUNDS
        outs = run_round(
            sources, widths, first_slots, factor_slots, sec_local, phys_count, size, final
        )
        if not final:
            packed = from_behind(outs[0], "site", 1)
            factor_slots = exchange(place(packed, slots, groups))
    isometry, upper = outs
    return isometry.reshape(1, sec_local, phys_count, size, size), upper[None]


def solution(mesh):
    in_specs = (P("site", "sec", None, None, None), P("site", "sec", None, None), P(), P())
    out_specs = (P("site", "sec", None, None, None), P("site", "sec", None, None))
    return jax.shard_map(body, mesh=mesh, in_specs=in_specs, out_specs=out_specs, check_vma=False)
```

```python
import functools
import math

import jax
import jax.numpy as jnp
from jax import lax
from jax.experimental import pallas as pl
from jax.experimental.pallas import tpu as pltpu
from jax.sharding import PartitionSpec as P

ROUNDS = 3
F32 = jnp.float32
BF16 = jnp.bfloat16
TILE = 128
HIGHEST = lax.Precision.HIGHEST


def contract(left, right, left_dim, right_dim, precision=None):
    dims = (((left_dim,), (right_dim,)), ((), ()))
    return lax.dot_general(left, right, dims, precision=precision, preferred_element_type=F32)


def from_behind(shard, axis, by):
    size = lax.axis_size(axis)
    return lax.ppermute(shard, axis, [(i, (i + by) % size) for i in range(size)])


class Packing:
    SPARE = 16

    def __init__(self, tiles):
        self.tiles = tiles
        self.row = {}
        at = 0
        for k in range(tiles):
            for q in range(k + 1, tiles):
                self.row[k, q] = at
                at += TILE
        for pair in range(tiles // 2):
            self.row[pair] = at
            at += TILE
        self.diagonals = at
        self.rows = at + self.SPARE


def ids():
    row_id = lax.broadcasted_iota(jnp.int32, (TILE, TILE), 0)
    column_id = lax.broadcasted_iota(jnp.int32, (TILE, TILE), 1)
    return row_id, column_id


def pack_pair(even, odd, row_id, column_id):
    return jnp.where(row_id <= column_id, even, jnp.transpose(odd)).astype(BF16)


def pack_diagonals(odds, row_id, column_id):
    spare = lax.broadcasted_iota(jnp.int32, (Packing.SPARE, TILE), 0)
    rows = jnp.zeros((Packing.SPARE, TILE), F32)
    for pair, odd in enumerate(odds):
        diagonal = jnp.sum(jnp.where(row_id == column_id, odd, 0.0), axis=0, keepdims=True)
        rows = jnp.where(spare == pair, jnp.broadcast_to(diagonal, rows.shape), rows)
    return rows.astype(BF16)


def unpack_diagonals(packing, held, row_id, column_id):
    diagonals = held[packing.diagonals : packing.diagonals + Packing.SPARE, :].astype(F32)
    tiles = []
    for pair in range(packing.tiles // 2):
        at = packing.row[pair]
        both = held[at : at + TILE, :].astype(F32)
        diagonal = jnp.broadcast_to(diagonals[pair : pair + 1, :], both.shape)
        odd = jnp.where(
            row_id > column_id, both, jnp.where(row_id == column_id, diagonal, 0.0)
        )
        tiles.append(jnp.where(row_id <= column_id, both, 0.0).astype(BF16))
        tiles.append(jnp.transpose(odd).astype(BF16))
    return tiles


def start_all(copies):
    for copy in copies:
        copy.start()
    return copies


def wait_all(copies):
    for copy in copies:
        copy.wait()


def place_first_kernel(
    unique, count, tiles, slot_ref, factor_ref, block_ref, out_ref,
    square, held, packed, factor_sem, read_sem, write_sem, packed_sem,
):
    packing = Packing(tiles)
    size = tiles * TILE
    row_id, column_id = ids()
    factor_reads = start_all(
        [pltpu.make_async_copy(factor_ref.at[u], square.at[u], factor_sem.at[u]) for u in range(unique)]
    )
    reads = start_all(
        [pltpu.make_async_copy(block_ref.at[g], held.at[g], read_sem.at[g]) for g in range(count)]
    )
    writes = []
    share = count // unique
    for u in range(unique):
        factor_reads[u].wait()
        tile = {}
        for k in range(tiles):
            for q in range(k, tiles):
                tile[k, q] = square[u, k * TILE : (k + 1) * TILE, q * TILE : (q + 1) * TILE]
                if q > k:
                    at = packing.row[k, q]
                    packed[u, at : at + TILE, :] = tile[k, q].astype(BF16)
        for pair in range(tiles // 2):
            at = packing.row[pair]
            even, odd = tile[2 * pair, 2 * pair], tile[2 * pair + 1, 2 * pair + 1]
            packed[u, at : at + TILE, :] = pack_pair(even, odd, row_id, column_id)
        odds = [tile[k, k] for k in range(1, tiles, 2)]
        packed[u, packing.diagonals :, :] = pack_diagonals(odds, row_id, column_id)
    for g in range(count):
        reads[g].wait()
        slot = slot_ref[g]
        for q in range(tiles):
            writes.append(
                pltpu.make_async_copy(
                    held.at[g, :, q * TILE : (q + 1) * TILE],
                    out_ref.at[slot, q * size : (q + 1) * size, :],
                    write_sem.at[g, q],
                )
            )
            writes[-1].start()
        writes.append(
            pltpu.make_async_copy(
                packed.at[g // share],
                out_ref.at[slot, tiles * size : tiles * size + packing.rows, :],
                packed_sem.at[g],
            )
        )
        writes[-1].start()
    wait_all(writes)


def place_first(blocks, factors, slots, groups):
    count, size, _ = blocks.shape
    unique = factors.shape[0]
    tiles = size // TILE
    packing = Packing(tiles)
    anywhere = pl.BlockSpec(memory_space=pl.ANY)
    return pl.pallas_call(
        functools.partial(place_first_kernel, unique, count, tiles),
        out_shape=jax.ShapeDtypeStruct((groups, tiles * size + packing.rows, TILE), BF16),
        in_specs=[pl.BlockSpec(memory_space=pltpu.SMEM), anywhere, anywhere],
        out_specs=anywhere,
        scratch_shapes=[
            pltpu.VMEM(factors.shape, F32),
            pltpu.VMEM(blocks.shape, BF16),
            pltpu.VMEM((unique, packing.rows, TILE), BF16),
            pltpu.SemaphoreType.DMA((unique,)),
            pltpu.SemaphoreType.DMA((count,)),
            pltpu.SemaphoreType.DMA((count, tiles)),
            pltpu.SemaphoreType.DMA((count,)),
        ],
        name="place_first",
    )(slots, factors, blocks)


def place_kernel(unique, count, slot_ref, block_ref, out_ref, write_sem):
    share = count // unique
    wait_all(
        start_all(
            [
                pltpu.make_async_copy(
                    block_ref.at[g // share], out_ref.at[slot_ref[g]], write_sem.at[g]
                )
                for g in range(count)
            ]
        )
    )


def place(blocks, slots, groups):
    unique, rows, columns = blocks.shape
    count = slots.shape[0]
    return pl.pallas_call(
        functools.partial(place_kernel, unique, count),
        out_shape=jax.ShapeDtypeStruct((groups, rows, columns), blocks.dtype),
        in_specs=[
            pl.BlockSpec(memory_space=pltpu.SMEM),
            pl.BlockSpec(memory_space=pltpu.VMEM),
        ],
        out_specs=pl.BlockSpec(memory_space=pl.ANY),
        scratch_shapes=[
            pltpu.SemaphoreType.DMA((count,)),
        ],
        name="place",
    )(slots, blocks)


def factor_group(rows8, j, lane, sub):
    full = (8, TILE)
    rows = [jnp.broadcast_to(rows8[t : t + 1, :], full) for t in range(8)]
    units = [jnp.where(lane == j + t, 1.0, 0.0) for t in range(8)]
    columns = [jnp.broadcast_to(rows8[:, j + u : j + u + 1], full) for u in range(8)]
    block = [
        [jnp.broadcast_to(columns[u][t : t + 1, :], full) if u >= t else None for u in range(8)]
        for t in range(8)
    ]
    inverse, lower = [], {}
    for t in range(8):
        inverse.append(1.0 / block[t][t])
        for u in range(t + 1, 8):
            lower[u, t] = block[t][u] * inverse[t]
        for u in range(t + 1, 8):
            for v in range(u, 8):
                block[u][v] = block[u][v] - lower[u, t] * block[t][v]
    for t in range(8):
        for v in range(t):
            rows[t] = rows[t] - lower[t, v] * rows[v]
            units[t] = units[t] - lower[t, v] * units[v]
    upper = jnp.zeros(full, F32)
    unit = jnp.zeros(full, F32)
    for t in range(8):
        root = lax.rsqrt(block[t][t])
        upper = jnp.where(sub == t, rows[t] * root, upper)
        unit = jnp.where(sub == t, units[t] * root, unit)
    reduced = [rows[t] * inverse[t] for t in range(8)]
    for t in range(7, -1, -1):
        for v in range(t + 1, 8):
            reduced[t] = reduced[t] - lower[v, t] * reduced[v]
    return upper, unit, reduced


def factor_tile(stacks):
    groups, wide = TILE // 8, 4
    lane = lax.broadcasted_iota(jnp.int32, (8, TILE), 1)
    sub = lax.broadcasted_iota(jnp.int32, (8, TILE), 0)
    uppers, units = [[] for _ in stacks], [[] for _ in stacks]
    for group in range(groups):
        j = group * 8
        end = (group // wide + 1) * wide
        for s, stack in enumerate(stacks):
            upper, unit, reduced = factor_group(stack[group], j, lane, sub)
            uppers[s].append(upper)
            units[s].append(unit)
            for i in range(group + 1, end):
                total = None
                for t in range(8):
                    term = jnp.broadcast_to(stack[i][:, j + t : j + t + 1], (8, TILE)) * reduced[t]
                    total = term if total is None else total + term
                stack[i] = stack[i] - total
        if end == group + 1 and end < groups:
            for s, stack in enumerate(stacks):
                done = jnp.concatenate(uppers[s][end - wide :], axis=0)
                update = contract(done, done, 0, 0, HIGHEST)
                for i in range(end, groups):
                    stack[i] = stack[i] - update[8 * i : 8 * i + 8]
    return uppers, units


def invert_tiles(uppers, units, row_id, column_id):
    span = 8
    while span < TILE:
        pair = (row_id // (2 * span) == column_id // (2 * span)) & (
            row_id // span != column_id // span
        )
        inner = [
            contract(unit, jnp.where(pair, upper, 0.0), 1, 1, HIGHEST)
            for upper, unit in zip(uppers, units)
        ]
        units = [unit - contract(part, unit, 1, 0, HIGHEST) for unit, part in zip(units, inner)]
        span *= 2
    return units


def round_kernel(sec_local, phys_count, tiles, shared, final, *refs):
    refs = list(refs)
    source_ref, width_ref, tensor_slots = refs[:3]
    factor_slots = tensor_slots if shared else refs[3]
    refs = refs[3 if shared else 4 :]
    outs, refs = refs[: 2 if final else 1], refs[2 if final else 1 :]
    tensors, factors, products, work, diag_inverse, tensor_sem, factor_sem = refs[:7]
    packing = Packing(tiles)
    size = tiles * TILE
    count = sec_local * phys_count
    row_id, column_id = ids()
    if final:
        isometry_ref, upper_out = outs
        upper_ref, full, high, low, staged, upper_sem, isometry_sem = refs[7:]
    else:
        packed_ref = outs[0]
    at_factor = tiles * size if shared else 0

    def tensor_copy(g, q):
        return pltpu.make_async_copy(
            tensor_slots.at[source_ref[g], q * size : (q + 1) * size, :],
            tensors.at[g, :, q * TILE : (q + 1) * TILE],
            tensor_sem.at[g, q],
        )

    def factor_copy(g):
        return pltpu.make_async_copy(
            factor_slots.at[source_ref[g], at_factor : at_factor + packing.rows, :],
            factors.at[g],
            factor_sem.at[g],
        )

    for g in range(count):
        factor_copy(g).start()
        for q in range(tiles):
            tensor_copy(g, q).start()

    def multiply(g, carry):
        factor_copy(g).wait()
        for q in range(tiles):
            tensor_copy(g, q).wait()
        held = factors.at[g]
        diagonal = unpack_diagonals(packing, held, row_id, column_id)
        for k in range(tiles):
            row = [diagonal[k]]
            for q in range(k + 1, tiles):
                at = packing.row[k, q]
                row.append(held[at : at + TILE, :])
            row = jnp.concatenate(row, axis=1) if len(row) > 1 else row[0]
            part = contract(row, tensors[g, k * TILE :, :], 1, 0)
            products[g, k * TILE : (k + 1) * TILE, :] = part.astype(BF16)
        return carry

    lax.fori_loop(0, count, multiply, 0)
    half = size // 2

    def gram(s, carry):
        stacked = products[pl.ds(s * phys_count, phys_count)].reshape(phys_count * size, size)
        work[s, :half, :] = contract(stacked[:, :half], stacked, 0, 0)
        work[s, half:, half:] = contract(stacked[:, half:], stacked[:, half:], 0, 0)
        for k in range(tiles):
            lo, hi = k * TILE, (k + 1) * TILE
            on = (row_id == column_id) & (row_id + lo >= width_ref[s])
            work[s, lo:hi, lo:hi] = work[s, lo:hi, lo:hi] + jnp.where(on, 1.0, 0.0)
        if final:
            upper_ref[s] = jnp.zeros((size, size), F32)
        return carry

    lax.fori_loop(0, sec_local, gram, 0)

    def step(p, carry):
        first = pl.multiple_of(p * TILE, TILE)
        stacks = []
        for s in range(sec_local):
            stacks.append(
                [
                    work[s, pl.ds(pl.multiple_of(first + 8 * i, 8), 8), pl.ds(first, TILE)]
                    for i in range(TILE // 8)
                ]
            )
        upper_rows, unit_rows = factor_tile(stacks)
        uppers = [
            jnp.where(row_id <= column_id, jnp.concatenate(rows, axis=0), 0.0)
            for rows in upper_rows
        ]
        units = [jnp.concatenate(rows, axis=0) for rows in unit_rows]
        inverses = invert_tiles(uppers, units, row_id, column_id)
        if final:
            for s in range(sec_local):
                diag_inverse[s, pl.ds(first, TILE), :] = inverses[s]
        else:
            for s in range(sec_local):
                diag_inverse[s, pl.ds(first, TILE), :] = uppers[s]
        for k in range(tiles):

            @pl.when(p == k)
            def _(k=k):
                lo, hi = k * TILE, (k + 1) * TILE
                for s in range(sec_local):
                    if final:
                        upper_ref[s, lo:hi, lo:hi] = uppers[s]
                    if k + 1 == tiles:
                        continue
                    panel = contract(inverses[s], work[s, lo:hi, hi:], 1, 0, HIGHEST)
                    for q in range(k + 1, tiles):
                        left = (q - k - 1) * TILE
                        piece = panel[:, left : left + TILE]
                        if final:
                            upper_ref[s, lo:hi, q * TILE : (q + 1) * TILE] = piece
                        else:
                            at = packing.row[k, q]
                            packed_ref[s, at : at + TILE, :] = piece.astype(BF16)
                        here = slice(q * TILE, (q + 1) * TILE)
                        work[s, here, q * TILE :] = work[s, here, q * TILE :] - contract(
                            piece, panel[:, left:], 0, 0, HIGHEST
                        )

        return carry

    lax.fori_loop(0, tiles, step, 0)
    if not final:
        for s in range(sec_local):
            diagonal = [diag_inverse[s, k * TILE : (k + 1) * TILE, :] for k in range(tiles)]
            for pair in range(tiles // 2):
                at = packing.row[pair]
                packed_ref[s, at : at + TILE, :] = pack_pair(
                    diagonal[2 * pair], diagonal[2 * pair + 1], row_id, column_id
                )
            packed_ref[s, packing.diagonals :, :] = pack_diagonals(
                diagonal[1::2], row_id, column_id
            )
        return
    uppers_out = start_all(
        [
            pltpu.make_async_copy(upper_ref.at[s], upper_out.at[s], upper_sem.at[s])
            for s in range(sec_local)
        ]
    )
    scale = math.sqrt(phys_count * size)

    def invert(s, carry):
        inverse = full.at[s]
        for k in range(tiles):
            lo, hi = k * TILE, (k + 1) * TILE
            inverse[lo:hi, lo:hi] = jnp.transpose(diag_inverse[s, lo:hi, :])
        span = TILE
        while span < size:
            for lo in range(0, size, 2 * span):
                mid, hi = lo + span, lo + 2 * span
                inner = contract(
                    upper_ref[s, lo:mid, mid:hi], inverse[mid:hi, mid:hi], 1, 0, HIGHEST
                )
                inverse[lo:mid, mid:hi] = -contract(inverse[lo:mid, lo:mid], inner, 1, 0, HIGHEST)
                inverse[mid:hi, lo:mid] = jnp.zeros((span, span), F32)
            span *= 2
        scaled = full[s] * scale
        rounded = scaled.astype(BF16)
        high[s] = rounded
        low[s] = (scaled - rounded.astype(F32)).astype(BF16)
        return carry

    lax.fori_loop(0, sec_local, invert, 0)

    def isometry_copy(g):
        return pltpu.make_async_copy(staged.at[g], isometry_ref.at[g], isometry_sem.at[g])

    def multiply_back(g, carry):
        s = g // phys_count
        for lo in range(0, size, 2 * TILE):
            hi = lo + 2 * TILE
            left = products[g, :, :hi]
            staged[g, :, lo:hi] = contract(left, high[s, :hi, lo:hi], 1, 0) + contract(
                left, low[s, :hi, lo:hi], 1, 0
            )
        isometry_copy(g).start()
        return carry

    lax.fori_loop(0, count, multiply_back, 0)
    wait_all(uppers_out + [isometry_copy(g) for g in range(count)])


def run_round(sources, widths, tensor_slots, factor_slots, sec_local, phys_count, size, final):
    tiles = size // TILE
    packing = Packing(tiles)
    count = sec_local * phys_count
    anywhere = pl.BlockSpec(memory_space=pl.ANY)
    smem = pl.BlockSpec(memory_space=pltpu.SMEM)
    shared = factor_slots is None
    operands = [sources, widths, tensor_slots] + ([] if shared else [factor_slots])
    scratch = [
        pltpu.VMEM((count, size, size), BF16),
        pltpu.VMEM((count, packing.rows, TILE), BF16),
        pltpu.VMEM((count, size, size), BF16),
        pltpu.VMEM((sec_local, size, size), F32),
        pltpu.VMEM((sec_local, size, TILE), F32),
        pltpu.SemaphoreType.DMA((count, tiles)),
        pltpu.SemaphoreType.DMA((count,)),
    ]
    if final:
        out_shape = [
            jax.ShapeDtypeStruct((count, size, size), F32),
            jax.ShapeDtypeStruct((sec_local, size, size), F32),
        ]
        out_specs = [anywhere, anywhere]
        scratch += [
            pltpu.VMEM((sec_local, size, size), F32),
            pltpu.VMEM((sec_local, size, size), F32),
            pltpu.VMEM((sec_local, size, size), BF16),
            pltpu.VMEM((sec_local, size, size), BF16),
            pltpu.VMEM((count, size, size), F32),
            pltpu.SemaphoreType.DMA((sec_local,)),
            pltpu.SemaphoreType.DMA((count,)),
        ]
    else:
        out_shape = [jax.ShapeDtypeStruct((sec_local, packing.rows, TILE), BF16)]
        out_specs = [pl.BlockSpec(memory_space=pltpu.VMEM)]
    return pl.pallas_call(
        functools.partial(round_kernel, sec_local, phys_count, tiles, shared, final),
        out_shape=out_shape,
        in_specs=[smem, smem] + [anywhere] * (len(operands) - 2),
        out_specs=out_specs,
        scratch_shapes=scratch,
        name="last_round" if final else "round",
    )(*operands)


def body(tensors, factors, sector_sizes, merging):
    site_index = lax.axis_index("site")
    sec_index = lax.axis_index("sec")
    site_count = lax.axis_size("site")
    groups = lax.axis_size("sec")
    blocks = tensors[0]
    sec_local, phys_count, size = blocks.shape[0], blocks.shape[1], blocks.shape[3]
    count = sec_local * phys_count
    rows = lax.dynamic_index_in_dim(merging, site_index, 0, keepdims=False)
    next_widths = lax.dynamic_index_in_dim(
        sector_sizes, (site_index + 1) % site_count, 0, keepdims=False
    )
    first = sec_index * sec_local
    widths = lax.dynamic_slice_in_dim(next_widths, first, sec_local)
    slots = lax.dynamic_slice_in_dim(rows, first, sec_local).reshape(count) // sec_local
    wanted = rows[None] == (first + jnp.arange(sec_local, dtype=jnp.int32))[:, None, None]
    order = jnp.arange(rows.shape[0], dtype=jnp.int32)[None, :, None]
    lefts = jnp.sum(jnp.where(wanted, order, 0), axis=1).reshape(count)
    slots, sources, widths = lax.optimization_barrier((slots, lefts // sec_local, widths))

    def exchange(slotted):
        return lax.all_to_all(slotted, "sec", split_axis=0, concat_axis=0, tiled=True)

    first_slots = exchange(
        place_first(blocks.reshape(count, size, size), factors[0], slots, groups)
    )
    factor_slots = None
    for round_index in range(ROUNDS):
        final = round_index + 1 == ROUNDS
        outs = run_round(
            sources, widths, first_slots, factor_slots, sec_local, phys_count, size, final
        )
        if not final:
            packed = from_behind(outs[0], "site", 1)
            factor_slots = exchange(place(packed, slots, groups))
    isometry, upper = outs
    return isometry.reshape(1, sec_local, phys_count, size, size), upper[None]


def solution(mesh):
    in_specs = (P("site", "sec", None, None, None), P("site", "sec", None, None), P(), P())
    out_specs = (P("site", "sec", None, None, None), P("site", "sec", None, None))
    return jax.shard_map(body, mesh=mesh, in_specs=in_specs, out_specs=out_specs, check_vma=False)
```

```python
import functools
import math

import jax
import jax.numpy as jnp
from jax import lax
from jax.experimental import pallas as pl
from jax.experimental.pallas import tpu as pltpu
from jax.sharding import PartitionSpec as P

ROUNDS = 3
F32 = jnp.float32
BF16 = jnp.bfloat16
TILE = 128
BLOCK = 32
HIGHEST = lax.Precision.HIGHEST


def contract(left, right, left_dim, right_dim, precision=None):
    dims = (((left_dim,), (right_dim,)), ((), ()))
    return lax.dot_general(left, right, dims, precision=precision, preferred_element_type=F32)


def from_behind(shard, axis, by):
    size = lax.axis_size(axis)
    return lax.ppermute(shard, axis, [(i, (i + by) % size) for i in range(size)])


class Packing:
    SPARE = 16

    def __init__(self, tiles):
        self.tiles = tiles
        self.row = {}
        at = 0
        for k in range(tiles):
            for q in range(k + 1, tiles):
                self.row[k, q] = at
                at += TILE
        for pair in range(tiles // 2):
            self.row[pair] = at
            at += TILE
        self.diagonals = at
        self.rows = at + self.SPARE


def ids():
    row_id = lax.broadcasted_iota(jnp.int32, (TILE, TILE), 0)
    column_id = lax.broadcasted_iota(jnp.int32, (TILE, TILE), 1)
    return row_id, column_id


def pack_pair(even, odd, row_id, column_id):
    return jnp.where(row_id <= column_id, even, jnp.transpose(odd)).astype(BF16)


def pack_diagonals(odds, row_id, column_id):
    spare = lax.broadcasted_iota(jnp.int32, (Packing.SPARE, TILE), 0)
    rows = jnp.zeros((Packing.SPARE, TILE), F32)
    for pair, odd in enumerate(odds):
        diagonal = jnp.sum(jnp.where(row_id == column_id, odd, 0.0), axis=0, keepdims=True)
        rows = jnp.where(spare == pair, jnp.broadcast_to(diagonal, rows.shape), rows)
    return rows.astype(BF16)


def unpack_diagonals(packing, held, row_id, column_id):
    diagonals = held[packing.diagonals : packing.diagonals + Packing.SPARE, :].astype(F32)
    tiles = []
    for pair in range(packing.tiles // 2):
        at = packing.row[pair]
        both = held[at : at + TILE, :].astype(F32)
        diagonal = jnp.broadcast_to(diagonals[pair : pair + 1, :], both.shape)
        odd = jnp.where(
            row_id > column_id, both, jnp.where(row_id == column_id, diagonal, 0.0)
        )
        tiles.append(jnp.where(row_id <= column_id, both, 0.0).astype(BF16))
        tiles.append(jnp.transpose(odd).astype(BF16))
    return tiles


def start_all(copies):
    for copy in copies:
        copy.start()
    return copies


def wait_all(copies):
    for copy in copies:
        copy.wait()


def place_first_kernel(
    unique, count, tiles, slot_ref, factor_ref, block_ref, out_ref,
    square, held, packed, factor_sem, read_sem, write_sem, packed_sem,
):
    packing = Packing(tiles)
    size = tiles * TILE
    row_id, column_id = ids()
    factor_reads = start_all(
        [pltpu.make_async_copy(factor_ref.at[u], square.at[u], factor_sem.at[u]) for u in range(unique)]
    )
    reads = start_all(
        [pltpu.make_async_copy(block_ref.at[g], held.at[g], read_sem.at[g]) for g in range(count)]
    )
    writes = []
    share = count // unique
    for u in range(unique):
        factor_reads[u].wait()
        tile = {}
        for k in range(tiles):
            for q in range(k, tiles):
                tile[k, q] = square[u, k * TILE : (k + 1) * TILE, q * TILE : (q + 1) * TILE]
                if q > k:
                    at = packing.row[k, q]
                    packed[u, at : at + TILE, :] = tile[k, q].astype(BF16)
        for pair in range(tiles // 2):
            at = packing.row[pair]
            even, odd = tile[2 * pair, 2 * pair], tile[2 * pair + 1, 2 * pair + 1]
            packed[u, at : at + TILE, :] = pack_pair(even, odd, row_id, column_id)
        odds = [tile[k, k] for k in range(1, tiles, 2)]
        packed[u, packing.diagonals :, :] = pack_diagonals(odds, row_id, column_id)
    for g in range(count):
        reads[g].wait()
        slot = slot_ref[g]
        for q in range(tiles):
            writes.append(
                pltpu.make_async_copy(
                    held.at[g, :, q * TILE : (q + 1) * TILE],
                    out_ref.at[slot, q * size : (q + 1) * size, :],
                    write_sem.at[g, q],
                )
            )
            writes[-1].start()
        writes.append(
            pltpu.make_async_copy(
                packed.at[g // share],
                out_ref.at[slot, tiles * size : tiles * size + packing.rows, :],
                packed_sem.at[g],
            )
        )
        writes[-1].start()
    wait_all(writes)


def place_first(blocks, factors, slots, groups):
    count, size, _ = blocks.shape
    unique = factors.shape[0]
    tiles = size // TILE
    packing = Packing(tiles)
    anywhere = pl.BlockSpec(memory_space=pl.ANY)
    return pl.pallas_call(
        functools.partial(place_first_kernel, unique, count, tiles),
        out_shape=jax.ShapeDtypeStruct((groups, tiles * size + packing.rows, TILE), BF16),
        in_specs=[pl.BlockSpec(memory_space=pltpu.SMEM), anywhere, anywhere],
        out_specs=anywhere,
        scratch_shapes=[
            pltpu.VMEM(factors.shape, F32),
            pltpu.VMEM(blocks.shape, BF16),
            pltpu.VMEM((unique, packing.rows, TILE), BF16),
            pltpu.SemaphoreType.DMA((unique,)),
            pltpu.SemaphoreType.DMA((count,)),
            pltpu.SemaphoreType.DMA((count, tiles)),
            pltpu.SemaphoreType.DMA((count,)),
        ],
        name="place_first",
    )(slots, factors, blocks)


def place_kernel(unique, count, slot_ref, block_ref, out_ref, write_sem):
    share = count // unique
    wait_all(
        start_all(
            [
                pltpu.make_async_copy(
                    block_ref.at[g // share], out_ref.at[slot_ref[g]], write_sem.at[g]
                )
                for g in range(count)
            ]
        )
    )


def place(blocks, slots, groups):
    unique, rows, columns = blocks.shape
    count = slots.shape[0]
    return pl.pallas_call(
        functools.partial(place_kernel, unique, count),
        out_shape=jax.ShapeDtypeStruct((groups, rows, columns), blocks.dtype),
        in_specs=[
            pl.BlockSpec(memory_space=pltpu.SMEM),
            pl.BlockSpec(memory_space=pltpu.VMEM),
        ],
        out_specs=pl.BlockSpec(memory_space=pl.ANY),
        scratch_shapes=[
            pltpu.SemaphoreType.DMA((count,)),
        ],
        name="place",
    )(slots, blocks)


def factor_group(rows8, units8, j, lane, sub):
    full = (8, TILE)
    rows = [jnp.broadcast_to(rows8[t : t + 1, :], full) for t in range(8)]
    units = [jnp.broadcast_to(units8[t : t + 1, :], full) for t in range(8)]
    columns = [jnp.broadcast_to(rows8[:, j + u : j + u + 1], full) for u in range(8)]
    block = [
        [jnp.broadcast_to(columns[u][t : t + 1, :], full) if u >= t else None for u in range(8)]
        for t in range(8)
    ]
    inverse, lower = [], {}
    for t in range(8):
        inverse.append(1.0 / block[t][t])
        for u in range(t + 1, 8):
            lower[u, t] = block[t][u] * inverse[t]
        for u in range(t + 1, 8):
            for v in range(u, 8):
                block[u][v] = block[u][v] - lower[u, t] * block[t][v]
    for t in range(8):
        for v in range(t):
            rows[t] = rows[t] - lower[t, v] * rows[v]
            units[t] = units[t] - lower[t, v] * units[v]
    upper = jnp.zeros(full, F32)
    unit = jnp.zeros(full, F32)
    for t in range(8):
        root = lax.rsqrt(block[t][t])
        upper = jnp.where(sub == t, rows[t] * root, upper)
        unit = jnp.where(sub == t, units[t] * root, unit)
    reduced = [rows[t] * inverse[t] for t in range(8)]
    reduced_units = [units[t] * inverse[t] for t in range(8)]
    for t in range(7, -1, -1):
        for v in range(t + 1, 8):
            reduced[t] = reduced[t] - lower[v, t] * reduced[v]
            reduced_units[t] = reduced_units[t] - lower[v, t] * reduced_units[v]
    return upper, unit, reduced, reduced_units


def factor_tile(stacks):
    groups, wide = TILE // 8, BLOCK // 8
    lane = lax.broadcasted_iota(jnp.int32, (8, TILE), 1)
    sub = lax.broadcasted_iota(jnp.int32, (8, TILE), 0)
    uppers, units = [[] for _ in stacks], [[] for _ in stacks]
    eyes = [[jnp.where(lane == 8 * i + sub, 1.0, 0.0) for i in range(groups)] for _ in stacks]
    for group in range(groups):
        j = group * 8
        end = (group // wide + 1) * wide
        for s, stack in enumerate(stacks):
            eye = eyes[s]
            upper, unit, reduced, reduced_units = factor_group(
                stack[group], eye[group], j, lane, sub
            )
            uppers[s].append(upper)
            units[s].append(unit)
            for i in range(group + 1, end):
                total, total_unit = None, None
                for t in range(8):
                    column = jnp.broadcast_to(stack[i][:, j + t : j + t + 1], (8, TILE))
                    term, term_unit = column * reduced[t], column * reduced_units[t]
                    total = term if total is None else total + term
                    total_unit = term_unit if total_unit is None else total_unit + term_unit
                stack[i] = stack[i] - total
                eye[i] = eye[i] - total_unit
        if end == group + 1 and end < groups:
            for s, stack in enumerate(stacks):
                done = jnp.concatenate(uppers[s][end - wide :], axis=0)
                update = contract(done, done, 0, 0, HIGHEST)
                for i in range(end, groups):
                    stack[i] = stack[i] - update[8 * i : 8 * i + 8]
    return uppers, units


def invert_tiles(uppers, units, row_id, column_id):
    span = BLOCK
    while span < TILE:
        pair = (row_id // (2 * span) == column_id // (2 * span)) & (
            row_id // span != column_id // span
        )
        inner = [
            contract(unit, jnp.where(pair, upper, 0.0), 1, 1, HIGHEST)
            for upper, unit in zip(uppers, units)
        ]
        units = [unit - contract(part, unit, 1, 0, HIGHEST) for unit, part in zip(units, inner)]
        span *= 2
    return units


def round_kernel(sec_local, phys_count, tiles, shared, final, *refs):
    refs = list(refs)
    source_ref, width_ref, tensor_slots = refs[:3]
    factor_slots = tensor_slots if shared else refs[3]
    refs = refs[3 if shared else 4 :]
    outs, refs = refs[: 2 if final else 1], refs[2 if final else 1 :]
    tensors, factors, products, work, diag_inverse, tensor_sem, factor_sem = refs[:7]
    packing = Packing(tiles)
    size = tiles * TILE
    count = sec_local * phys_count
    row_id, column_id = ids()
    if final:
        isometry_ref, upper_out = outs
        upper_ref, full, high, low, staged, upper_sem, isometry_sem = refs[7:]
    else:
        packed_ref = outs[0]
    at_factor = tiles * size if shared else 0

    def tensor_copy(g, q):
        return pltpu.make_async_copy(
            tensor_slots.at[source_ref[g], q * size : (q + 1) * size, :],
            tensors.at[g, :, q * TILE : (q + 1) * TILE],
            tensor_sem.at[g, q],
        )

    def factor_copy(g):
        return pltpu.make_async_copy(
            factor_slots.at[source_ref[g], at_factor : at_factor + packing.rows, :],
            factors.at[g],
            factor_sem.at[g],
        )

    for g in range(count):
        factor_copy(g).start()
        for q in range(tiles):
            tensor_copy(g, q).start()

    def multiply(g, carry):
        factor_copy(g).wait()
        for q in range(tiles):
            tensor_copy(g, q).wait()
        held = factors.at[g]
        diagonal = unpack_diagonals(packing, held, row_id, column_id)
        for k in range(tiles):
            row = [diagonal[k]]
            for q in range(k + 1, tiles):
                at = packing.row[k, q]
                row.append(held[at : at + TILE, :])
            row = jnp.concatenate(row, axis=1) if len(row) > 1 else row[0]
            part = contract(row, tensors[g, k * TILE :, :], 1, 0)
            products[g, k * TILE : (k + 1) * TILE, :] = part.astype(BF16)
        return carry

    lax.fori_loop(0, count, multiply, 0)
    half = size // 2

    def gram(s, carry):
        stacked = products[pl.ds(s * phys_count, phys_count)].reshape(phys_count * size, size)
        work[s, :half, :] = contract(stacked[:, :half], stacked, 0, 0)
        work[s, half:, half:] = contract(stacked[:, half:], stacked[:, half:], 0, 0)
        for k in range(tiles):
            lo, hi = k * TILE, (k + 1) * TILE
            on = (row_id == column_id) & (row_id + lo >= width_ref[s])
            work[s, lo:hi, lo:hi] = work[s, lo:hi, lo:hi] + jnp.where(on, 1.0, 0.0)
        if final:
            upper_ref[s] = jnp.zeros((size, size), F32)
        return carry

    lax.fori_loop(0, sec_local, gram, 0)

    def step(p, carry):
        first = pl.multiple_of(p * TILE, TILE)
        stacks = []
        for s in range(sec_local):
            stacks.append(
                [
                    work[s, pl.ds(pl.multiple_of(first + 8 * i, 8), 8), pl.ds(first, TILE)]
                    for i in range(TILE // 8)
                ]
            )
        upper_rows, unit_rows = factor_tile(stacks)
        uppers = [
            jnp.where(row_id <= column_id, jnp.concatenate(rows, axis=0), 0.0)
            for rows in upper_rows
        ]
        units = [jnp.concatenate(rows, axis=0) for rows in unit_rows]
        inverses = invert_tiles(uppers, units, row_id, column_id)
        if final:
            for s in range(sec_local):
                diag_inverse[s, pl.ds(first, TILE), :] = inverses[s]
        else:
            for s in range(sec_local):
                diag_inverse[s, pl.ds(first, TILE), :] = uppers[s]
        for k in range(tiles):

            @pl.when(p == k)
            def _(k=k):
                lo, hi = k * TILE, (k + 1) * TILE
                for s in range(sec_local):
                    if final:
                        upper_ref[s, lo:hi, lo:hi] = uppers[s]
                    if k + 1 == tiles:
                        continue
                    panel = contract(inverses[s], work[s, lo:hi, hi:], 1, 0, HIGHEST)
                    for q in range(k + 1, tiles):
                        left = (q - k - 1) * TILE
                        piece = panel[:, left : left + TILE]
                        if final:
                            upper_ref[s, lo:hi, q * TILE : (q + 1) * TILE] = piece
                        else:
                            at = packing.row[k, q]
                            packed_ref[s, at : at + TILE, :] = piece.astype(BF16)
                        here = slice(q * TILE, (q + 1) * TILE)
                        work[s, here, q * TILE :] = work[s, here, q * TILE :] - contract(
                            piece, panel[:, left:], 0, 0, HIGHEST
                        )

        return carry

    lax.fori_loop(0, tiles, step, 0)
    if not final:
        for s in range(sec_local):
            diagonal = [diag_inverse[s, k * TILE : (k + 1) * TILE, :] for k in range(tiles)]
            for pair in range(tiles // 2):
                at = packing.row[pair]
                packed_ref[s, at : at + TILE, :] = pack_pair(
                    diagonal[2 * pair], diagonal[2 * pair + 1], row_id, column_id
                )
            packed_ref[s, packing.diagonals :, :] = pack_diagonals(
                diagonal[1::2], row_id, column_id
            )
        return
    uppers_out = start_all(
        [
            pltpu.make_async_copy(upper_ref.at[s], upper_out.at[s], upper_sem.at[s])
            for s in range(sec_local)
        ]
    )
    scale = math.sqrt(phys_count * size)

    def invert(s, carry):
        inverse = full.at[s]
        for k in range(tiles):
            lo, hi = k * TILE, (k + 1) * TILE
            inverse[lo:hi, lo:hi] = jnp.transpose(diag_inverse[s, lo:hi, :])
        span = TILE
        while span < size:
            for lo in range(0, size, 2 * span):
                mid, hi = lo + span, lo + 2 * span
                inner = contract(
                    upper_ref[s, lo:mid, mid:hi], inverse[mid:hi, mid:hi], 1, 0, HIGHEST
                )
                inverse[lo:mid, mid:hi] = -contract(inverse[lo:mid, lo:mid], inner, 1, 0, HIGHEST)
                inverse[mid:hi, lo:mid] = jnp.zeros((span, span), F32)
            span *= 2
        scaled = full[s] * scale
        rounded = scaled.astype(BF16)
        high[s] = rounded
        low[s] = (scaled - rounded.astype(F32)).astype(BF16)
        return carry

    lax.fori_loop(0, sec_local, invert, 0)

    def isometry_copy(g):
        return pltpu.make_async_copy(staged.at[g], isometry_ref.at[g], isometry_sem.at[g])

    def multiply_back(g, carry):
        s = g // phys_count
        for lo in range(0, size, 2 * TILE):
            hi = lo + 2 * TILE
            left = products[g, :, :hi]
            staged[g, :, lo:hi] = contract(left, high[s, :hi, lo:hi], 1, 0) + contract(
                left, low[s, :hi, lo:hi], 1, 0
            )
        isometry_copy(g).start()
        return carry

    lax.fori_loop(0, count, multiply_back, 0)
    wait_all(uppers_out + [isometry_copy(g) for g in range(count)])


def run_round(sources, widths, tensor_slots, factor_slots, sec_local, phys_count, size, final):
    tiles = size // TILE
    packing = Packing(tiles)
    count = sec_local * phys_count
    anywhere = pl.BlockSpec(memory_space=pl.ANY)
    smem = pl.BlockSpec(memory_space=pltpu.SMEM)
    shared = factor_slots is None
    operands = [sources, widths, tensor_slots] + ([] if shared else [factor_slots])
    scratch = [
        pltpu.VMEM((count, size, size), BF16),
        pltpu.VMEM((count, packing.rows, TILE), BF16),
        pltpu.VMEM((count, size, size), BF16),
        pltpu.VMEM((sec_local, size, size), F32),
        pltpu.VMEM((sec_local, size, TILE), F32),
        pltpu.SemaphoreType.DMA((count, tiles)),
        pltpu.SemaphoreType.DMA((count,)),
    ]
    if final:
        out_shape = [
            jax.ShapeDtypeStruct((count, size, size), F32),
            jax.ShapeDtypeStruct((sec_local, size, size), F32),
        ]
        out_specs = [anywhere, anywhere]
        scratch += [
            pltpu.VMEM((sec_local, size, size), F32),
            pltpu.VMEM((sec_local, size, size), F32),
            pltpu.VMEM((sec_local, size, size), BF16),
            pltpu.VMEM((sec_local, size, size), BF16),
            pltpu.VMEM((count, size, size), F32),
            pltpu.SemaphoreType.DMA((sec_local,)),
            pltpu.SemaphoreType.DMA((count,)),
        ]
    else:
        out_shape = [jax.ShapeDtypeStruct((sec_local, packing.rows, TILE), BF16)]
        out_specs = [pl.BlockSpec(memory_space=pltpu.VMEM)]
    return pl.pallas_call(
        functools.partial(round_kernel, sec_local, phys_count, tiles, shared, final),
        out_shape=out_shape,
        in_specs=[smem, smem] + [anywhere] * (len(operands) - 2),
        out_specs=out_specs,
        scratch_shapes=scratch,
        name="last_round" if final else "round",
    )(*operands)


def body(tensors, factors, sector_sizes, merging):
    site_index = lax.axis_index("site")
    sec_index = lax.axis_index("sec")
    site_count = lax.axis_size("site")
    groups = lax.axis_size("sec")
    blocks = tensors[0]
    sec_local, phys_count, size = blocks.shape[0], blocks.shape[1], blocks.shape[3]
    count = sec_local * phys_count
    rows = lax.dynamic_index_in_dim(merging, site_index, 0, keepdims=False)
    next_widths = lax.dynamic_index_in_dim(
        sector_sizes, (site_index + 1) % site_count, 0, keepdims=False
    )
    first = sec_index * sec_local
    widths = lax.dynamic_slice_in_dim(next_widths, first, sec_local)
    slots = lax.dynamic_slice_in_dim(rows, first, sec_local).reshape(count) // sec_local
    wanted = rows[None] == (first + jnp.arange(sec_local, dtype=jnp.int32))[:, None, None]
    order = jnp.arange(rows.shape[0], dtype=jnp.int32)[None, :, None]
    lefts = jnp.sum(jnp.where(wanted, order, 0), axis=1).reshape(count)
    slots, sources, widths = lax.optimization_barrier((slots, lefts // sec_local, widths))

    def exchange(slotted):
        return lax.all_to_all(slotted, "sec", split_axis=0, concat_axis=0, tiled=True)

    first_slots = exchange(
        place_first(blocks.reshape(count, size, size), factors[0], slots, groups)
    )
    factor_slots = None
    for round_index in range(ROUNDS):
        final = round_index + 1 == ROUNDS
        outs = run_round(
            sources, widths, first_slots, factor_slots, sec_local, phys_count, size, final
        )
        if not final:
            packed = from_behind(outs[0], "site", 1)
            factor_slots = exchange(place(packed, slots, groups))
    isometry, upper = outs
    return isometry.reshape(1, sec_local, phys_count, size, size), upper[None]


def solution(mesh):
    in_specs = (P("site", "sec", None, None, None), P("site", "sec", None, None), P(), P())
    out_specs = (P("site", "sec", None, None, None), P("site", "sec", None, None))
    return jax.shard_map(body, mesh=mesh, in_specs=in_specs, out_specs=out_specs, check_vma=False)
```

```python
import functools
import math

import jax
import jax.numpy as jnp
from jax import lax
from jax.experimental import pallas as pl
from jax.experimental.pallas import tpu as pltpu
from jax.sharding import PartitionSpec as P

ROUNDS = 3
F32 = jnp.float32
BF16 = jnp.bfloat16
TILE = 128
BLOCK = 32
HIGHEST = lax.Precision.HIGHEST


def contract(left, right, left_dim, right_dim, precision=None):
    dims = (((left_dim,), (right_dim,)), ((), ()))
    return lax.dot_general(left, right, dims, precision=precision, preferred_element_type=F32)


def from_behind(shard, axis, by):
    size = lax.axis_size(axis)
    return lax.ppermute(shard, axis, [(i, (i + by) % size) for i in range(size)])


class Packing:
    SPARE = 16

    def __init__(self, tiles):
        self.tiles = tiles
        self.row = {}
        at = 0
        for k in range(tiles):
            for q in range(k + 1, tiles):
                self.row[k, q] = at
                at += TILE
        for pair in range(tiles // 2):
            self.row[pair] = at
            at += TILE
        self.diagonals = at
        self.rows = at + self.SPARE


def ids():
    row_id = lax.broadcasted_iota(jnp.int32, (TILE, TILE), 0)
    column_id = lax.broadcasted_iota(jnp.int32, (TILE, TILE), 1)
    return row_id, column_id


def pack_pair(even, odd, row_id, column_id):
    return jnp.where(row_id <= column_id, even, jnp.transpose(odd)).astype(BF16)


def pack_diagonals(odds, row_id, column_id):
    spare = lax.broadcasted_iota(jnp.int32, (Packing.SPARE, TILE), 0)
    rows = jnp.zeros((Packing.SPARE, TILE), F32)
    for pair, odd in enumerate(odds):
        diagonal = jnp.sum(jnp.where(row_id == column_id, odd, 0.0), axis=0, keepdims=True)
        rows = jnp.where(spare == pair, jnp.broadcast_to(diagonal, rows.shape), rows)
    return rows.astype(BF16)


def unpack_diagonals(packing, held, row_id, column_id):
    diagonals = held[packing.diagonals : packing.diagonals + Packing.SPARE, :].astype(F32)
    tiles = []
    for pair in range(packing.tiles // 2):
        at = packing.row[pair]
        both = held[at : at + TILE, :].astype(F32)
        diagonal = jnp.broadcast_to(diagonals[pair : pair + 1, :], both.shape)
        odd = jnp.where(
            row_id > column_id, both, jnp.where(row_id == column_id, diagonal, 0.0)
        )
        tiles.append(jnp.where(row_id <= column_id, both, 0.0).astype(BF16))
        tiles.append(jnp.transpose(odd).astype(BF16))
    return tiles


def start_all(copies):
    for copy in copies:
        copy.start()
    return copies


def wait_all(copies):
    for copy in copies:
        copy.wait()


def place_first_kernel(
    unique, count, tiles, slot_ref, factor_ref, block_ref, out_ref,
    square, held, packed, factor_sem, read_sem, write_sem, packed_sem,
):
    packing = Packing(tiles)
    size = tiles * TILE
    row_id, column_id = ids()
    factor_reads = start_all(
        [pltpu.make_async_copy(factor_ref.at[u], square.at[u], factor_sem.at[u]) for u in range(unique)]
    )
    reads = start_all(
        [pltpu.make_async_copy(block_ref.at[g], held.at[g], read_sem.at[g]) for g in range(count)]
    )
    writes = []
    share = count // unique
    for u in range(unique):
        factor_reads[u].wait()
        tile = {}
        for k in range(tiles):
            for q in range(k, tiles):
                tile[k, q] = square[u, k * TILE : (k + 1) * TILE, q * TILE : (q + 1) * TILE]
                if q > k:
                    at = packing.row[k, q]
                    packed[u, at : at + TILE, :] = tile[k, q].astype(BF16)
        for pair in range(tiles // 2):
            at = packing.row[pair]
            even, odd = tile[2 * pair, 2 * pair], tile[2 * pair + 1, 2 * pair + 1]
            packed[u, at : at + TILE, :] = pack_pair(even, odd, row_id, column_id)
        odds = [tile[k, k] for k in range(1, tiles, 2)]
        packed[u, packing.diagonals :, :] = pack_diagonals(odds, row_id, column_id)
    for g in range(count):
        reads[g].wait()
        slot = slot_ref[g]
        for q in range(tiles):
            writes.append(
                pltpu.make_async_copy(
                    held.at[g, :, q * TILE : (q + 1) * TILE],
                    out_ref.at[slot, q * size : (q + 1) * size, :],
                    write_sem.at[g, q],
                )
            )
            writes[-1].start()
        writes.append(
            pltpu.make_async_copy(
                packed.at[g // share],
                out_ref.at[slot, tiles * size : tiles * size + packing.rows, :],
                packed_sem.at[g],
            )
        )
        writes[-1].start()
    wait_all(writes)


def place_first(blocks, factors, slots, groups):
    count, size, _ = blocks.shape
    unique = factors.shape[0]
    tiles = size // TILE
    packing = Packing(tiles)
    anywhere = pl.BlockSpec(memory_space=pl.ANY)
    return pl.pallas_call(
        functools.partial(place_first_kernel, unique, count, tiles),
        out_shape=jax.ShapeDtypeStruct((groups, tiles * size + packing.rows, TILE), BF16),
        in_specs=[pl.BlockSpec(memory_space=pltpu.SMEM), anywhere, anywhere],
        out_specs=anywhere,
        scratch_shapes=[
            pltpu.VMEM(factors.shape, F32),
            pltpu.VMEM(blocks.shape, BF16),
            pltpu.VMEM((unique, packing.rows, TILE), BF16),
            pltpu.SemaphoreType.DMA((unique,)),
            pltpu.SemaphoreType.DMA((count,)),
            pltpu.SemaphoreType.DMA((count, tiles)),
            pltpu.SemaphoreType.DMA((count,)),
        ],
        compiler_params=pltpu.CompilerParams(vmem_limit_bytes=16 * 2**20),
        name="place_first",
    )(slots, factors, blocks)


def place_kernel(unique, count, slot_ref, block_ref, out_ref, write_sem):
    share = count // unique
    wait_all(
        start_all(
            [
                pltpu.make_async_copy(
                    block_ref.at[g // share], out_ref.at[slot_ref[g]], write_sem.at[g]
                )
                for g in range(count)
            ]
        )
    )


def place(blocks, slots, groups):
    unique, rows, columns = blocks.shape
    count = slots.shape[0]
    return pl.pallas_call(
        functools.partial(place_kernel, unique, count),
        out_shape=jax.ShapeDtypeStruct((groups, rows, columns), blocks.dtype),
        in_specs=[
            pl.BlockSpec(memory_space=pltpu.SMEM),
            pl.BlockSpec(memory_space=pltpu.VMEM),
        ],
        out_specs=pl.BlockSpec(memory_space=pl.ANY),
        scratch_shapes=[
            pltpu.SemaphoreType.DMA((count,)),
        ],
        compiler_params=pltpu.CompilerParams(vmem_limit_bytes=8 * 2**20),
        name="place",
    )(slots, blocks)


def factor_group(rows8, units8, j, lane, sub):
    full = (8, TILE)
    rows = [jnp.broadcast_to(rows8[t : t + 1, :], full) for t in range(8)]
    units = [jnp.broadcast_to(units8[t : t + 1, :], full) for t in range(8)]
    columns = [jnp.broadcast_to(rows8[:, j + u : j + u + 1], full) for u in range(8)]
    block = [
        [jnp.broadcast_to(columns[u][t : t + 1, :], full) if u >= t else None for u in range(8)]
        for t in range(8)
    ]
    inverse, lower = [], {}
    for t in range(8):
        inverse.append(1.0 / block[t][t])
        for u in range(t + 1, 8):
            lower[u, t] = block[t][u] * inverse[t]
        for u in range(t + 1, 8):
            for v in range(u, 8):
                block[u][v] = block[u][v] - lower[u, t] * block[t][v]
    for t in range(8):
        for v in range(t):
            rows[t] = rows[t] - lower[t, v] * rows[v]
            units[t] = units[t] - lower[t, v] * units[v]
    upper = jnp.zeros(full, F32)
    unit = jnp.zeros(full, F32)
    for t in range(8):
        root = lax.rsqrt(block[t][t])
        upper = jnp.where(sub == t, rows[t] * root, upper)
        unit = jnp.where(sub == t, units[t] * root, unit)
    reduced = [rows[t] * inverse[t] for t in range(8)]
    reduced_units = [units[t] * inverse[t] for t in range(8)]
    for t in range(7, -1, -1):
        for v in range(t + 1, 8):
            reduced[t] = reduced[t] - lower[v, t] * reduced[v]
            reduced_units[t] = reduced_units[t] - lower[v, t] * reduced_units[v]
    return upper, unit, reduced, reduced_units


def factor_tile(stacks):
    groups, wide = TILE // 8, BLOCK // 8
    lane = lax.broadcasted_iota(jnp.int32, (8, TILE), 1)
    sub = lax.broadcasted_iota(jnp.int32, (8, TILE), 0)
    uppers, units = [[] for _ in stacks], [[] for _ in stacks]
    eyes = [[jnp.where(lane == 8 * i + sub, 1.0, 0.0) for i in range(groups)] for _ in stacks]
    for group in range(groups):
        j = group * 8
        end = (group // wide + 1) * wide
        for s, stack in enumerate(stacks):
            eye = eyes[s]
            upper, unit, reduced, reduced_units = factor_group(
                stack[group], eye[group], j, lane, sub
            )
            uppers[s].append(upper)
            units[s].append(unit)
            for i in range(group + 1, end):
                total, total_unit = None, None
                for t in range(8):
                    column = jnp.broadcast_to(stack[i][:, j + t : j + t + 1], (8, TILE))
                    term, term_unit = column * reduced[t], column * reduced_units[t]
                    total = term if total is None else total + term
                    total_unit = term_unit if total_unit is None else total_unit + term_unit
                stack[i] = stack[i] - total
                eye[i] = eye[i] - total_unit
        if end == group + 1 and end < groups:
            for s, stack in enumerate(stacks):
                done = jnp.concatenate(uppers[s][end - wide :], axis=0)
                update = contract(done, done, 0, 0, HIGHEST)
                for i in range(end, groups):
                    stack[i] = stack[i] - update[8 * i : 8 * i + 8]
    return uppers, units


def invert_tiles(uppers, units, row_id, column_id):
    span = BLOCK
    while span < TILE:
        pair = (row_id // (2 * span) == column_id // (2 * span)) & (
            row_id // span != column_id // span
        )
        inner = [
            contract(unit, jnp.where(pair, upper, 0.0), 1, 1, HIGHEST)
            for upper, unit in zip(uppers, units)
        ]
        units = [unit - contract(part, unit, 1, 0, HIGHEST) for unit, part in zip(units, inner)]
        span *= 2
    return units


def round_kernel(sec_local, phys_count, tiles, shared, final, *refs):
    refs = list(refs)
    source_ref, width_ref, tensor_slots = refs[:3]
    factor_slots = tensor_slots if shared else refs[3]
    refs = refs[3 if shared else 4 :]
    n_outs = 2 if final or shared else 1
    outs, refs = refs[:n_outs], refs[n_outs:]
    if shared:
        tensors = outs[1]
    else:
        tensors = tensor_slots
    factors, products, work, diag_inverse, tensor_sem, factor_sem = refs[:6]
    packing = Packing(tiles)
    size = tiles * TILE
    count = sec_local * phys_count
    row_id, column_id = ids()
    if final:
        isometry_ref, upper_out = outs
        upper_ref, full, high, low, staged, upper_sem, isometry_sem = refs[6:]
    else:
        packed_ref = outs[0]
    at_factor = tiles * size if shared else 0

    def tensor_copy(g, q):
        return pltpu.make_async_copy(
            tensor_slots.at[source_ref[g], q * size : (q + 1) * size, :],
            tensors.at[g, :, q * TILE : (q + 1) * TILE],
            tensor_sem.at[g, q],
        )

    def factor_copy(g):
        return pltpu.make_async_copy(
            factor_slots.at[source_ref[g], at_factor : at_factor + packing.rows, :],
            factors.at[g],
            factor_sem.at[g],
        )

    for g in range(count):
        factor_copy(g).start()
        if shared:
            for q in range(tiles):
                tensor_copy(g, q).start()

    def multiply(g, carry):
        factor_copy(g).wait()
        if shared:
            for q in range(tiles):
                tensor_copy(g, q).wait()
        held = factors.at[g]
        diagonal = unpack_diagonals(packing, held, row_id, column_id)
        for k in range(tiles):
            row = [diagonal[k]]
            for q in range(k + 1, tiles):
                at = packing.row[k, q]
                row.append(held[at : at + TILE, :])
            row = jnp.concatenate(row, axis=1) if len(row) > 1 else row[0]
            part = contract(row, tensors[g, k * TILE :, :], 1, 0)
            products[g, k * TILE : (k + 1) * TILE, :] = part.astype(BF16)
        return carry

    lax.fori_loop(0, count, multiply, 0)
    half = size // 2

    def gram(s, carry):
        stacked = products[pl.ds(s * phys_count, phys_count)].reshape(phys_count * size, size)
        work[s, :half, :] = contract(stacked[:, :half], stacked, 0, 0)
        work[s, half:, half:] = contract(stacked[:, half:], stacked[:, half:], 0, 0)
        for k in range(tiles):
            lo, hi = k * TILE, (k + 1) * TILE
            on = (row_id == column_id) & (row_id + lo >= width_ref[s])
            work[s, lo:hi, lo:hi] = work[s, lo:hi, lo:hi] + jnp.where(on, 1.0, 0.0)
        if final:
            upper_ref[s] = jnp.zeros((size, size), F32)
        return carry

    lax.fori_loop(0, sec_local, gram, 0)

    def step(p, carry):
        first = pl.multiple_of(p * TILE, TILE)
        stacks = []
        for s in range(sec_local):
            stacks.append(
                [
                    work[s, pl.ds(pl.multiple_of(first + 8 * i, 8), 8), pl.ds(first, TILE)]
                    for i in range(TILE // 8)
                ]
            )
        upper_rows, unit_rows = factor_tile(stacks)
        uppers = [
            jnp.where(row_id <= column_id, jnp.concatenate(rows, axis=0), 0.0)
            for rows in upper_rows
        ]
        units = [jnp.concatenate(rows, axis=0) for rows in unit_rows]
        inverses = invert_tiles(uppers, units, row_id, column_id)
        if final:
            for s in range(sec_local):
                diag_inverse[s, pl.ds(first, TILE), :] = inverses[s]
        else:
            for s in range(sec_local):
                diag_inverse[s, pl.ds(first, TILE), :] = uppers[s]
        for k in range(tiles):

            @pl.when(p == k)
            def _(k=k):
                lo, hi = k * TILE, (k + 1) * TILE
                for s in range(sec_local):
                    if final:
                        upper_ref[s, lo:hi, lo:hi] = uppers[s]
                    if k + 1 == tiles:
                        continue
                    panel = contract(inverses[s], work[s, lo:hi, hi:], 1, 0, HIGHEST)
                    for q in range(k + 1, tiles):
                        left = (q - k - 1) * TILE
                        piece = panel[:, left : left + TILE]
                        if final:
                            upper_ref[s, lo:hi, q * TILE : (q + 1) * TILE] = piece
                        else:
                            at = packing.row[k, q]
                            packed_ref[s, at : at + TILE, :] = piece.astype(BF16)
                        here = slice(q * TILE, (q + 1) * TILE)
                        work[s, here, q * TILE :] = work[s, here, q * TILE :] - contract(
                            piece, panel[:, left:], 0, 0, HIGHEST
                        )

        return carry

    lax.fori_loop(0, tiles, step, 0)
    if not final:
        for s in range(sec_local):
            diagonal = [diag_inverse[s, k * TILE : (k + 1) * TILE, :] for k in range(tiles)]
            for pair in range(tiles // 2):
                at = packing.row[pair]
                packed_ref[s, at : at + TILE, :] = pack_pair(
                    diagonal[2 * pair], diagonal[2 * pair + 1], row_id, column_id
                )
            packed_ref[s, packing.diagonals :, :] = pack_diagonals(
                diagonal[1::2], row_id, column_id
            )
        return
    uppers_out = start_all(
        [
            pltpu.make_async_copy(upper_ref.at[s], upper_out.at[s], upper_sem.at[s])
            for s in range(sec_local)
        ]
    )
    scale = math.sqrt(phys_count * size)

    def invert(s, carry):
        inverse = full.at[s]
        for k in range(tiles):
            lo, hi = k * TILE, (k + 1) * TILE
            inverse[lo:hi, lo:hi] = jnp.transpose(diag_inverse[s, lo:hi, :])
        span = TILE
        while span < size:
            for lo in range(0, size, 2 * span):
                mid, hi = lo + span, lo + 2 * span
                inner = contract(
                    upper_ref[s, lo:mid, mid:hi], inverse[mid:hi, mid:hi], 1, 0, HIGHEST
                )
                inverse[lo:mid, mid:hi] = -contract(inverse[lo:mid, lo:mid], inner, 1, 0, HIGHEST)
                inverse[mid:hi, lo:mid] = jnp.zeros((span, span), F32)
            span *= 2
        scaled = full[s] * scale
        rounded = scaled.astype(BF16)
        high[s] = rounded
        low[s] = (scaled - rounded.astype(F32)).astype(BF16)
        return carry

    lax.fori_loop(0, sec_local, invert, 0)

    def isometry_copy(g):
        return pltpu.make_async_copy(staged.at[g], isometry_ref.at[g], isometry_sem.at[g])

    def multiply_back(g, carry):
        s = g // phys_count
        for lo in range(0, size, 2 * TILE):
            hi = lo + 2 * TILE
            left = products[g, :, :hi]
            staged[g, :, lo:hi] = contract(left, high[s, :hi, lo:hi], 1, 0) + contract(
                left, low[s, :hi, lo:hi], 1, 0
            )
        isometry_copy(g).start()
        return carry

    lax.fori_loop(0, count, multiply_back, 0)
    wait_all(uppers_out + [isometry_copy(g) for g in range(count)])


def run_round(sources, widths, tensor_slots, factor_slots, sec_local, phys_count, size, final):
    tiles = size // TILE
    packing = Packing(tiles)
    count = sec_local * phys_count
    anywhere = pl.BlockSpec(memory_space=pl.ANY)
    smem = pl.BlockSpec(memory_space=pltpu.SMEM)
    vmem = pl.BlockSpec(memory_space=pltpu.VMEM)
    shared = factor_slots is None
    operands = [sources, widths, tensor_slots] + ([] if shared else [factor_slots])
    scratch = [
        pltpu.VMEM((count, packing.rows, TILE), BF16),
        pltpu.VMEM((count, size, size), BF16),
        pltpu.VMEM((sec_local, size, size), F32),
        pltpu.VMEM((sec_local, size, TILE), F32),
        pltpu.SemaphoreType.DMA((count, tiles)),
        pltpu.SemaphoreType.DMA((count,)),
    ]
    if final:
        out_shape = [
            jax.ShapeDtypeStruct((count, size, size), F32),
            jax.ShapeDtypeStruct((sec_local, size, size), F32),
        ]
        out_specs = [anywhere, anywhere]
        scratch += [
            pltpu.VMEM((sec_local, size, size), F32),
            pltpu.VMEM((sec_local, size, size), F32),
            pltpu.VMEM((sec_local, size, size), BF16),
            pltpu.VMEM((sec_local, size, size), BF16),
            pltpu.VMEM((count, size, size), F32),
            pltpu.SemaphoreType.DMA((sec_local,)),
            pltpu.SemaphoreType.DMA((count,)),
        ]
    else:
        out_shape = [jax.ShapeDtypeStruct((sec_local, packing.rows, TILE), BF16)]
        out_specs = [pl.BlockSpec(memory_space=pltpu.VMEM)]
        if shared:
            out_shape.append(pltpu.VMEM((count, size, size), BF16))
            out_specs.append(pl.BlockSpec(memory_space=pltpu.VMEM))
    return pl.pallas_call(
        functools.partial(round_kernel, sec_local, phys_count, tiles, shared, final),
        out_shape=out_shape,
        in_specs=[smem, smem] + ([anywhere] if shared else [vmem, anywhere]),
        out_specs=out_specs,
        scratch_shapes=scratch,
        compiler_params=pltpu.CompilerParams(vmem_limit_bytes=40 * 2**20),
        name="last_round" if final else "round",
    )(*operands)


def body(tensors, factors, sector_sizes, merging):
    site_index = lax.axis_index("site")
    sec_index = lax.axis_index("sec")
    site_count = lax.axis_size("site")
    groups = lax.axis_size("sec")
    blocks = tensors[0]
    sec_local, phys_count, size = blocks.shape[0], blocks.shape[1], blocks.shape[3]
    count = sec_local * phys_count
    rows = lax.dynamic_index_in_dim(merging, site_index, 0, keepdims=False)
    next_widths = lax.dynamic_index_in_dim(
        sector_sizes, (site_index + 1) % site_count, 0, keepdims=False
    )
    first = sec_index * sec_local
    widths = lax.dynamic_slice_in_dim(next_widths, first, sec_local)
    slots = lax.dynamic_slice_in_dim(rows, first, sec_local).reshape(count) // sec_local
    wanted = rows[None] == (first + jnp.arange(sec_local, dtype=jnp.int32))[:, None, None]
    order = jnp.arange(rows.shape[0], dtype=jnp.int32)[None, :, None]
    lefts = jnp.sum(jnp.where(wanted, order, 0), axis=1).reshape(count)
    slots, sources, widths = lax.optimization_barrier((slots, lefts // sec_local, widths))

    def exchange(slotted):
        return lax.all_to_all(slotted, "sec", split_axis=0, concat_axis=0, tiled=True)

    first_slots = exchange(
        place_first(blocks.reshape(count, size, size), factors[0], slots, groups)
    )
    factor_slots = None
    for round_index in range(ROUNDS):
        final = round_index + 1 == ROUNDS
        outs = run_round(
            sources, widths, first_slots, factor_slots, sec_local, phys_count, size, final
        )
        if round_index == 0:
            first_slots = outs[1]
        if not final:
            packed = from_behind(outs[0], "site", 1)
            factor_slots = exchange(place(packed, slots, groups))
    isometry, upper = outs
    return isometry.reshape(1, sec_local, phys_count, size, size), upper[None]


def solution(mesh):
    in_specs = (P("site", "sec", None, None, None), P("site", "sec", None, None), P(), P())
    out_specs = (P("site", "sec", None, None, None), P("site", "sec", None, None))
    return jax.shard_map(body, mesh=mesh, in_specs=in_specs, out_specs=out_specs, check_vma=False)
```
